256 devices in a mesh: lat: 8 (over y_hi, x), lon: 32 (over z, y_lo, core).
Axes of the slice: x: 4, y: 4 (y_hi: 2, y_lo: 2; y = y_hi * 2 + y_lo), z: 8, core: 2. Of those that a mesh axis runs over, the one named last changes fastest.
Arguments:
- target: float32 [3, 512, 16384], P(None, 'lat', 'lon'), may hold values from -8 to 8
- latent_0: float32 [512, 16384], P('lat', 'lon'), may hold values from -10 to 10
- latent_1: float32 [256, 8192], P('lat', 'lon'), may hold values from -10 to 10
- latent_2: float32 [128, 4096], P('lat', 'lon'), may hold values from -10 to 10
- latent_3: float32 [64, 2048], P('lat', 'lon'), may hold values from -10 to 10
- latent_4: float32 [32, 1024], P('lat', 'lon'), may hold values from -10 to 10
- latent_5: float32 [16, 512], P('lat', 'lon'), may hold values from -10 to 10
- tile_seeds: int32 [8, 32], P('lat', 'lon'), may hold values from 0 to 1073741823
- anchor_parity: int32 [6], replicated, may hold values from 0 to 1
- anchor_scale: float32 [6], replicated, may hold values from 0.5 to 4
- mix_levels: bfloat16 [24, 6], replicated, may hold values from -2.5 to 2.5
- mix_hidden: bfloat16 [24, 24], replicated, may hold values from -1.25 to 1.25
- conv_first: bfloat16 [24, 24, 3, 3], replicated, may hold values from -0.4375 to 0.4375
- conv_second: bfloat16 [24, 24, 3, 3], replicated, may hold values from -0.4375 to 0.4375
- conv_output: bfloat16 [3, 24, 3, 3], replicated, may hold values from -0.4375 to 0.4375
- context_in: float32 [24, 12], replicated, may hold values from -1.75 to 1.75
- context_mid: float32 [24, 24], replicated, may hold values from -1.25 to 1.25
- context_out: float32 [2, 24], replicated, may hold values from -1.25 to 1.25
Outputs:
- reconstruction: float32 [3, 512, 16384], P(None, 'lat', 'lon')
- bits_finest: float32 [512, 16384], P('lat', 'lon')
- loss_terms: float32 [7], replicated
- output_grad: float32 [3, 24, 3, 3], replicated
The draws below stay inside these ranges and needn't reach their ends.
All inputs are finite; a program needn't handle non-finite values.
Results may differ from the reference program's by a relative error of at most 0.00035.
The reference program's roundings to bfloat16 on the way (of `upsampled`, `first`, `second`, `third`, `fourth` and `slope`) count: a program that leaves them out, or rounds other values in their place, can miss the bound.
Values may be sent and summed in bfloat16 or wider, within the bound.
No kernel may reach another device: no remote copies, remote signals or barrier semaphores. Data moves between devices by JAX's collectives and lax.ppermute only.
A program may use at most 128 MiB of HBM per device.

```python
import math
import jax
import jax.numpy as jnp
from jax import lax

H_DEV = 64
W_DEV = 512
LEVELS = 6
CH = 24
ARM_WIDTH = 24
CTX = 12
BANDS = 3
NH = 512
NW = 16384
TILE_ROWS = 8
TILE_COLS = 32


def draw_target(key, part):
    first_key, second_key = jax.random.split(jax.random.fold_in(key, 11))
    rows_pos = jnp.arange(NH, dtype=jnp.float32) / NH
    cols_pos = jnp.arange(NW, dtype=jnp.float32) / NW
    trend = 0.4 * jnp.power(3.0, cols_pos)[None, None, :] * jnp.power(2.0, rows_pos)[None, :, None]
    rough = jax.random.uniform(second_key, (BANDS, NH, NW), jnp.float32, 0.5, 1.5)
    values = jax.random.normal(first_key, (BANDS, NH, NW), jnp.float32) * rough * trend
    return jnp.clip(values, -8.0, 8.0)


def with_ends(values, key, least, high):
    extent = values.shape
    place = [jax.random.randint(jax.random.fold_in(key, axis), (), 0, extent[axis]) for axis in range(len(extent))]
    values = values.at[tuple(place)].set(least)
    longest = extent.index(max(extent))
    place[longest] = (place[longest] + 1) % extent[longest]
    return values.at[tuple(place)].set(high)


def shard_levels(rng, dims, pieces, smallest, top_value):
    def one(dim, blocks):
        heights = jax.random.uniform(jax.random.fold_in(jax.random.fold_in(rng, 6), dim), (blocks,), jnp.float32, smallest / len(pieces), top_value / len(pieces))
        return jnp.repeat(jnp.exp(heights), dims[dim] // blocks).reshape((-1,) + (1,) * (len(dims) - dim - 1))

    level = one(*pieces[0])
    for cut in pieces[1:]:
        level = level * one(*cut)
    return level


def gaussian(own_key, shape, scale, reach, pieces=(), kind=jnp.bfloat16):
    level = shard_levels(own_key, shape, pieces, -0.22, 0.18) if pieces else 1.0
    values = jax.random.normal(own_key, shape, jnp.float32) * scale * level
    return jnp.minimum(jnp.maximum(values, -reach), reach).astype(kind)


def setup_inputs(seed: int = 0) -> dict:
    key_of = jax.random.split(jax.random.key(seed), 19)
    target = draw_target(jax.random.fold_in(key_of[18], 71), 0)
    latent_0 = gaussian(key_of[1], (NH, NW), 2.0, 10.0, ((0, 8), (1, 32)), jnp.float32)
    latent_1 = gaussian(key_of[2], (NH // 2, NW // 2), 2.0, 10.0, ((0, 8), (1, 32)), jnp.float32)
    latent_2 = gaussian(key_of[3], (NH // 4, NW // 4), 2.0, 10.0, ((0, 8), (1, 32)), jnp.float32)
    latent_3 = gaussian(key_of[4], (NH // 8, NW // 8), 2.0, 10.0, ((0, 8), (1, 32)), jnp.float32)
    latent_4 = gaussian(key_of[5], (NH // 16, NW // 16), 2.0, 10.0, ((0, 8), (1, 32)), jnp.float32)
    latent_5 = gaussian(key_of[6], (NH // 32, NW // 32), 2.0, 10.0, ((0, 8), (1, 32)), jnp.float32)
    tile_seeds = with_ends(jax.random.randint(key_of[7], (TILE_ROWS, TILE_COLS), 0, 1073741824), jax.random.fold_in(key_of[7], 1), 0, 1073741823).astype(jnp.int32)
    anchor_parity = with_ends(jax.random.randint(key_of[8], (LEVELS,), 0, 2), jax.random.fold_in(key_of[8], 1), 0, 1).astype(jnp.int32)
    anchor_scale = jnp.clip(jnp.exp(jax.random.uniform(key_of[9], (LEVELS,), jnp.float32, math.log(0.5), math.log(4.0))), 0.5, 4.0)
    mix_levels = gaussian(key_of[10], (CH, LEVELS), LEVELS ** -0.5, 2.5)
    mix_hidden = gaussian(key_of[11], (CH, CH), CH ** -0.5, 1.25)
    conv_first = gaussian(key_of[12], (CH, CH, 3, 3), (9 * CH) ** -0.5, 0.4375)
    conv_second = gaussian(key_of[13], (CH, CH, 3, 3), (9 * CH) ** -0.5, 0.4375)
    conv_output = gaussian(key_of[14], (BANDS, CH, 3, 3), (9 * CH) ** -0.5, 0.4375)
    context_in = gaussian(key_of[15], (ARM_WIDTH, CTX), CTX ** -0.5, 1.75, (), jnp.float32)
    context_mid = gaussian(key_of[16], (ARM_WIDTH, ARM_WIDTH), ARM_WIDTH ** -0.5, 1.25, (), jnp.float32)
    context_out = gaussian(key_of[17], (2, ARM_WIDTH), ARM_WIDTH ** -0.5, 1.25, (), jnp.float32)
    return {"target": target, "latent_0": latent_0, "latent_1": latent_1, "latent_2": latent_2, "latent_3": latent_3, "latent_4": latent_4, "latent_5": latent_5, "tile_seeds": tile_seeds, "anchor_parity": anchor_parity, "anchor_scale": anchor_scale, "mix_levels": mix_levels, "mix_hidden": mix_hidden, "conv_first": conv_first, "conv_second": conv_second, "conv_output": conv_output, "context_in": context_in, "context_mid": context_mid, "context_out": context_out}


mix_level = 668265263
mix_row = 374761393
mix_col = 1103515245
mix_mult = 73244475
log_two = 0.6931471805599453
context_steps = ((-1, 0), (1, 0), (0, -1), (0, 1), (-2, -1), (-2, 1), (2, -1), (2, 1), (-1, -2), (-1, 2), (1, -2), (1, 2))


def logical_shift(value, places):
    return jnp.bitwise_and(jnp.right_shift(value, jnp.int32(places)), jnp.int32((1 << (32 - places)) - 1))


def hashed_noise(seed_value, level_index, local_rows, local_cols):
    value = seed_value + jnp.int32(level_index) * jnp.int32(mix_level)
    value = value + local_rows[:, None] * jnp.int32(mix_row) + local_cols[None, :] * jnp.int32(mix_col)
    value = jnp.bitwise_xor(value, logical_shift(value, 15))
    value = value * jnp.int32(mix_mult)
    value = jnp.bitwise_xor(value, logical_shift(value, 13))
    value = value * jnp.int32(mix_mult)
    value = jnp.bitwise_xor(value, logical_shift(value, 16))
    return jnp.bitwise_and(value, jnp.int32(16777215)).astype(jnp.float32) / 16777216.0 - 0.5


def upsample_axis(extended, factor, along):
    cells_in = extended.shape[along] - 2
    earlier = lax.slice_in_dim(extended, 0, cells_in, axis=along)
    current = lax.slice_in_dim(extended, 1, cells_in + 1, axis=along)
    following = lax.slice_in_dim(extended, 2, cells_in + 2, axis=along)
    position = (jnp.arange(factor, dtype=jnp.float32) + 0.5) / factor - 0.5
    weight_low = jnp.maximum(-position, 0.0)
    weight_high = jnp.maximum(position, 0.0)
    weight_mid = 1.0 - weight_low - weight_high
    view_shape = [1] * (extended.ndim + 1)
    view_shape[along + 1] = factor
    result = jnp.expand_dims(earlier, along + 1) * weight_low.reshape(view_shape)
    result = result + jnp.expand_dims(current, along + 1) * weight_mid.reshape(view_shape)
    result = result + jnp.expand_dims(following, along + 1) * weight_high.reshape(view_shape)
    new_shape = list(extended.shape)
    new_shape[along] = cells_in * factor
    return result.reshape(new_shape)


def laplace_bits(offset, spread):
    magnitude = jnp.abs(offset)
    outer = jnp.log(0.5) - (jnp.maximum(magnitude, 0.5) - 0.5) / spread + jnp.log(-jnp.expm1(-1.0 / spread))
    inner_offset = jnp.clip(offset, -0.5, 0.5)
    inner = jnp.log(1.0 - 0.5 * (jnp.exp(-(0.5 - inner_offset) / spread) + jnp.exp(-(0.5 + inner_offset) / spread)))
    return -jnp.where(magnitude >= 0.5, outer, inner) / log_two


def level_bits(extended, context_in, context_mid, context_out, anchor_value, parity_bit, row_start, col_start):
    rows_in = extended.shape[0] - 4
    cols_in = extended.shape[1] - 4
    context = jnp.stack([extended[2 + row_step:2 + row_step + rows_in, 2 + col_step:2 + col_step + cols_in] for row_step, col_step in context_steps])
    quantized = extended[2:2 + rows_in, 2:2 + cols_in]
    highest = lax.Precision.HIGHEST
    inner = jax.nn.relu(jnp.einsum("hk,kyx->hyx", context_in, context, precision=highest))
    outer = jax.nn.relu(jnp.einsum("hg,gyx->hyx", context_mid, inner, precision=highest))
    raw_out = jnp.einsum("oh,hyx->oyx", context_out, outer, precision=highest)
    row_ids = row_start + jnp.arange(rows_in, dtype=jnp.int32)
    col_ids = col_start + jnp.arange(cols_in, dtype=jnp.int32)
    anchor = ((row_ids[:, None] + col_ids[None, :] + parity_bit) % 2) == 0
    centre = jnp.where(anchor, 0.0, raw_out[0])
    spread = jnp.where(anchor, anchor_value, 0.1 + jax.nn.softplus(raw_out[1]))
    return laplace_bits(quantized - centre, spread)


def conv_rows(field, kernel, row_pad):
    return lax.conv_general_dilated(field[None], kernel, (1, 1), ((row_pad, row_pad), (0, 0)), dimension_numbers=("NCHW", "OIHW", "NCHW"), preferred_element_type=jnp.float32)[0]


def reference(target, latent_0, latent_1, latent_2, latent_3, latent_4, latent_5, tile_seeds, anchor_parity, anchor_scale, mix_levels, mix_hidden, conv_first, conv_second, conv_output, context_in, context_mid, context_out):
    latents = (latent_0, latent_1, latent_2, latent_3, latent_4, latent_5)
    quantized_levels = []
    for level_index in range(LEVELS):
        tile_rows = H_DEV // 2 ** level_index
        tile_cols = W_DEV // 2 ** level_index
        row_ids = jnp.arange(NH // 2 ** level_index, dtype=jnp.int32)
        col_ids = jnp.arange(NW // 2 ** level_index, dtype=jnp.int32)
        seed_field = tile_seeds[(row_ids // tile_rows)[:, None], (col_ids // tile_cols)[None, :]]
        noise = hashed_noise(seed_field, level_index, row_ids % tile_rows, col_ids % tile_cols)
        quantized_levels.append(latents[level_index] + noise)
    pixel_count = BANDS * NH * NW

    def one_block(block_index):
        col_start = block_index * W_DEV
        up_layers = []
        bit_sums = []
        bits_top = None
        for level_index in range(LEVELS):
            factor = 2 ** level_index
            cols_level = W_DEV // factor
            total_cols = NW // factor
            spare = (3 + factor - 1) // factor
            column_ids = (block_index * cols_level + jnp.arange(-spare - 1, cols_level + spare + 1, dtype=jnp.int32)) % total_cols
            rowed = jnp.pad(jnp.take(quantized_levels[level_index], column_ids, axis=1), ((1, 1), (0, 0)))
            grown = upsample_axis(upsample_axis(rowed, factor, 0), factor, 1)
            margin = spare * factor - 3
            up_layers.append(grown[:, margin:margin + W_DEV + 6])
            near_ids = (block_index * cols_level + jnp.arange(-2, cols_level + 2, dtype=jnp.int32)) % total_cols
            extended = jnp.pad(jnp.take(quantized_levels[level_index], near_ids, axis=1), ((2, 2), (0, 0)))
            bits = level_bits(extended, context_in, context_mid, context_out, anchor_scale[level_index], anchor_parity[level_index], jnp.int32(0), block_index * cols_level)
            if level_index == 0:
                bits_top = bits
            bit_sums.append(jnp.sum(bits))
        upsampled = jnp.stack(up_layers).astype(jnp.bfloat16)
        first = jax.nn.relu(jnp.einsum("cl,lhw->chw", mix_levels, upsampled, preferred_element_type=jnp.float32)).astype(jnp.bfloat16)
        second = jax.nn.relu(jnp.einsum("cd,dhw->chw", mix_hidden, first, preferred_element_type=jnp.float32)).astype(jnp.bfloat16)
        third = (second[:, :, 1:-1] + jax.nn.relu(conv_rows(second, conv_first, 1))).astype(jnp.bfloat16)
        fourth = (third[:, :, 1:-1] + jax.nn.relu(conv_rows(third, conv_second, 1))).astype(jnp.bfloat16)
        padded = jnp.pad(fourth, ((0, 0), (1, 1), (0, 0)))
        recon = conv_rows(padded, conv_output, 0)
        error = recon - lax.dynamic_slice_in_dim(target, col_start, W_DEV, 2)
        squared = jnp.sum(error * error)
        slope = (2.0 * error / pixel_count).astype(jnp.bfloat16)
        taps = []
        for row_tap in range(3):
            for col_tap in range(3):
                window = padded[:, row_tap:row_tap + NH, col_tap:col_tap + W_DEV]
                taps.append(jnp.einsum("ohw,chw->oc", slope, window, preferred_element_type=jnp.float32))
        gradient = jnp.stack(taps, axis=-1).reshape(BANDS, slope.shape[0] * 0 + fourth.shape[0], 3, 3)
        return recon, bits_top, jnp.stack(bit_sums), squared, gradient

    recons, tops, level_sums, squares, gradients = lax.map(one_block, jnp.arange(NW // W_DEV, dtype=jnp.int32))
    reconstruction = recons.transpose(1, 2, 0, 3).reshape(BANDS, NH, NW)
    bits_finest = tops.transpose(1, 0, 2).reshape(NH, NW)
    cells = jnp.array([(NH // 2 ** level_index) * (NW // 2 ** level_index) for level_index in range(LEVELS)], dtype=jnp.float32)
    loss_terms = jnp.concatenate([jnp.sum(squares)[None] / pixel_count, jnp.sum(level_sums, axis=0) / cells])
    return reconstruction, bits_finest, loss_terms, jnp.sum(gradients, axis=0)
```

```python
import functools

import jax
import jax.numpy as jnp
import numpy as np
from jax import lax
from jax.experimental import pallas as pl
from jax.experimental.pallas import tpu as pltpu
from jax.sharding import PartitionSpec as P

F32, BF16, I32 = jnp.float32, jnp.bfloat16, jnp.int32
STEPS = (
    (-1, 0), (1, 0), (0, -1), (0, 1), (-2, -1), (-2, 1),
    (2, -1), (2, 1), (-1, -2), (-1, 2), (1, -2), (1, 2),
)
LEVELS, CH, H, W = 6, 24, 64, 512
ROWS = [H >> l for l in range(LEVELS)]
COLS = [W >> l for l in range(LEVELS)]
HALO = [3, 2, 2, 2, 2, 2]
OFFS = [0, 3, 5, 7, 9, 11]
PACK = 13
WIDE = [640, 384, 256, 128, 128, 128]
TALL = [80, 48, 32, 32, 32, 32]
TOP = 12
LANES = 640
BLOCKS = 9
BLOCK = 8 * CH
SLAB = 256
EDGE = 32
PLACE = [(0, 0), (3, 0), (3, 384), (5, 0), (5, 128), (5, 256)]
VMEM = pl.BlockSpec(memory_space=pltpu.VMEM)
SMEM = pl.BlockSpec(memory_space=pltpu.SMEM)


def dot(a, b):
    return lax.dot_general(a, b, (((1,), (0,)), ((), ())), preferred_element_type=F32)


def wrap32(v):
    return int(np.int64(v).astype(np.int32))


def quantize(lat_ref, seed, level):
    shape = lat_ref.shape
    rows = lax.broadcasted_iota(I32, shape, 0)
    cols = lax.broadcasted_iota(I32, shape, 1)
    h = (seed + wrap32(level * 668265263)) + rows * 374761393 + cols * 1103515245
    h = h ^ lax.shift_right_logical(h, jnp.full(shape, 15, I32))
    h = h * 73244475
    h = h ^ lax.shift_right_logical(h, jnp.full(shape, 13, I32))
    h = h * 73244475
    h = h ^ lax.shift_right_logical(h, jnp.full(shape, 16, I32))
    noise = (h & 16777215).astype(F32) * (1.0 / 16777216.0) - 0.5
    return lat_ref[...] + noise


def place_own(lats, seed, fields):
    for level in range(LEVELS):
        fields[level][...] = jnp.zeros(fields[level].shape, F32)
        fields[level][TOP : TOP + ROWS[level], 0 : COLS[level]] = quantize(
            lats[level], seed, level
        )


def place_sides(left, right, fields):
    lane = lax.broadcasted_iota(I32, (8, 128), 1)
    for level in range(LEVELS):
        h, c = HALO[level], COLS[level]
        start = c % 128
        base = (c // 128) * 128
        for g in range(max(1, ROWS[level] // 8)):
            at = PACK * g + OFFS[level]
            a = pltpu.roll(right, (start - at) % 128, 1)
            b = pltpu.roll(left, (128 - h - at) % 128, 1)
            tile = jnp.where((lane >= start) & (lane < start + h), a, 0.0)
            tile = jnp.where(lane >= 128 - h, b, tile)
            rows = pl.ds(TOP + 8 * g, 8)
            if level < 3:
                fields[level][rows, base : base + 128] = tile
            else:
                fields[level][rows, 0:128] = fields[level][rows, 0:128] + tile


def place_ends(above, below, fields):
    for level in range(LEVELS):
        h, (r, c), w = HALO[level], PLACE[level], WIDE[level]
        fields[level][TOP - h : TOP, :] = above[r : r + h, c : c + w]
        end = TOP + ROWS[level]
        fields[level][end : end + h, :] = below[r : r + h, c : c + w]


def sides_kernel(seed, *refs):
    lats, (to_right, to_left), fields = refs[:6], refs[6:8], refs[8:]
    place_own(lats, seed[0, 0], fields)
    lane = lax.broadcasted_iota(I32, (8, 128), 1)
    right = jnp.zeros((8, 128), F32)
    left = jnp.zeros((8, 128), F32)
    for level in range(LEVELS):
        h, c = HALO[level], COLS[level]
        base = max(c - 128, 0)
        for g in range(max(1, ROWS[level] // 8)):
            at = PACK * g + OFFS[level]
            here = (lane >= at) & (lane < at + h)
            rows = pl.ds(TOP + 8 * g, 8)
            last = fields[level][rows, base : base + 128]
            first = fields[level][rows, 0:128]
            right = jnp.where(here, pltpu.roll(last, (at - (c - h - base)) % 128, 1), right)
            left = jnp.where(here, pltpu.roll(first, at % 128, 1), left)
    to_right[...] = right
    to_left[...] = left


def ends_kernel(seed, *refs):
    lats, (left, right), (up, down), fields = refs[:6], refs[6:8], refs[8:10], refs[10:]
    place_own(lats, seed[0, 0], fields)
    place_sides(left[...], right[...], fields)
    up[...] = jnp.zeros(up.shape, F32)
    down[...] = jnp.zeros(down.shape, F32)
    for level in range(LEVELS):
        h, (r, c), w = HALO[level], PLACE[level], WIDE[level]
        end = TOP + ROWS[level]
        up[r : r + h, c : c + w] = fields[level][TOP : TOP + h, :]
        down[r : r + h, c : c + w] = fields[level][end - h : end, :]


def slab_row(d, c):
    return CH * d + EDGE + c


@functools.lru_cache(None)
def tables():
    t = {}
    spread = np.zeros((BLOCK, CH), np.float32)
    for r in range(8):
        for c in range(CH):
            spread[CH * r + c, c] = 1
    t["spread"] = spread
    t["gather"] = np.ascontiguousarray(spread.T)
    place = np.zeros((CH, SLAB), np.float32)
    tap = np.full((BLOCK, SLAB), 9, np.float32)
    for d in range(-1, 9):
        for c in range(CH):
            place[c, slab_row(d, c)] = 1
            for r in range(8):
                tap[CH * r : CH * r + CH, slab_row(d, c)] = d - r + 1
    t["place"], t["tap"] = place, tap
    t["tap_out"] = np.tile(tap[::CH], (3, 1))
    same = np.zeros((BLOCK, BLOCK), np.float32)
    for r in range(8):
        same[CH * r : CH * r + CH, CH * r : CH * r + CH] = 1
    t["same"] = same
    t["same_out"] = np.tile(same[::CH], (2, 1))
    levels = np.zeros((LEVELS, 8 * LEVELS), np.float32)
    rowof = np.zeros((BLOCK, 8 * LEVELS), np.float32)
    for l in range(LEVELS):
        for r in range(8):
            levels[l, 8 * l + r] = 1
            rowof[CH * r : CH * r + CH, 8 * l + r] = 1
    t["levels"], t["rowof"] = levels, rowof
    ctx = np.zeros((8, len(STEPS), 80), np.float32)
    for r in range(8):
        for k, (i, j) in enumerate(STEPS):
            ctx[r, k, (j + 2) * 16 + (r + i + 4)] = 1
    t["ctx"] = ctx
    for l in range(1, LEVELS):
        s = 1 << l
        up_r = np.zeros((80, TALL[l]), np.float32)
        for n in range(72):
            y = n - 4
            m, p = y >> l, ((y & (s - 1)) + 0.5) / s - 0.5
            for e, wgt in ((-1, max(-p, 0)), (0, 1 - abs(p)), (1, max(p, 0))):
                at = TOP + m + e
                if 0 <= at < TALL[l]:
                    up_r[n, at] += wgt
        up_c = np.zeros((WIDE[l], LANES), np.float32)
        for n in range(LANES):
            x = n if n < W + 4 else n - LANES
            if x < -4:
                continue
            m, p = x >> l, ((x & (s - 1)) + 0.5) / s - 0.5
            for e, wgt in ((-1, max(-p, 0)), (0, 1 - abs(p)), (1, max(p, 0))):
                q = m + e
                if -HALO[l] <= q < COLS[l] + HALO[l]:
                    up_c[q % WIDE[l], n] += wgt
        t[f"rows{l}"] = np.concatenate([up_r] * 3, axis=1)
        t[f"cols{l}"] = up_c
    return t


def table(name, dtype=BF16):
    return jnp.asarray(tables()[name], dtype)


def split2(x):
    hi = x.astype(BF16)
    return hi, (x - hi.astype(F32)).astype(BF16)


def split3(x):
    hi = x.astype(BF16)
    rest = x - hi.astype(F32)
    mid = rest.astype(BF16)
    return hi, mid, (rest - mid.astype(F32)).astype(BF16)


def weights_kernel(
    ml, mh, cf, cs, co, w1, w2, w3, spread, gather, place, tap, tap_out, same, same_out,
    levels, rowof, ctx, wm1, wm2, wc1, wc2, wout, a1, a2, a3,
):
    grow = spread[...]
    wide = gather[...]

    def diag(w):
        return dot(dot(grow, w).astype(BF16), wide) * same[...].astype(F32)

    wm1[...] = (
        dot(dot(grow, ml[...]).astype(BF16), levels[...]) * rowof[...].astype(F32)
    ).astype(BF16)
    wm2[...] = diag(mh[...]).astype(BF16)
    taps = tap[...].astype(F32)
    for src, dst in ((cf, wc1), (cs, wc2)):
        for b in range(3):
            total = jnp.zeros((BLOCK, SLAB), F32)
            for a in range(3):
                full = dot(dot(grow, src[a, b]).astype(BF16), place[...])
                total = jnp.where(taps == float(a), full, total)
            dst[BLOCK * b : BLOCK * b + BLOCK, :] = total.astype(BF16)
    rows = dot(co[...], place[...])
    taps3 = tap_out[...].astype(F32)[0:8]
    for b in range(3):
        for o in range(3):
            total = jnp.zeros((8, SLAB), F32)
            for a in range(3):
                k = 9 * o + 3 * a + b
                total = jnp.where(
                    taps3 == float(a), jnp.broadcast_to(rows[k : k + 1], (8, SLAB)), total
                )
            at = 24 * b + 8 * o
            wout[at : at + 8, :] = total
    hi, lo = split2(w1[...])
    for r in range(8):
        sel = ctx[r]
        h, l = dot(hi, sel).astype(BF16), dot(lo, sel).astype(BF16)
        a1[CH * r : CH * r + CH, :] = jnp.concatenate([h, h, l], axis=1)
    hi, lo = split2(w2[...])
    h, l = diag(hi).astype(BF16), diag(lo).astype(BF16)
    a2[...] = jnp.concatenate([h, h, l], axis=1)
    hi, lo = split2(w3[...])
    keep = same_out[...].astype(F32)

    def out(w):
        v = dot(w, wide)
        v = jnp.concatenate(
            [jnp.broadcast_to(v[0:1], (8, BLOCK)), jnp.broadcast_to(v[1:2], (8, BLOCK))], axis=0
        )
        return (v * keep).astype(BF16)

    h, l = out(hi), out(lo)
    a3[...] = jnp.concatenate([h, h, l], axis=1)


def laplace(x, centre, spread):
    y = 1.0 / spread
    off = x - centre
    mag = jnp.abs(off)
    inside = jnp.clip(off, -0.5, 0.5)
    e1 = jnp.exp((inside - 0.5) * y)
    e2 = jnp.exp((-0.5 - inside) * y)
    poly = y * (1 - y * (1 / 2 - y * (1 / 6 - y * (1 / 24 - y * (1 / 120)))))
    tail = jnp.where(y < 0.05, poly, 1.0 - e1 * e2)
    beyond = mag >= 0.5
    arg = jnp.where(beyond, 0.5 * tail, 1.0 - 0.5 * (e1 + e2))
    extra = jnp.where(beyond, (mag - 0.5) * y, 0.0)
    return (extra - jnp.log(arg)) * (1.0 / 0.6931471805599453)


def main_kernel(
    seed, parity, scale, ends, l0, l1, l2, l3, l4, l5, left, right, above, below, target,
    wm1, wm2, wc1, wc2, wout, a1, a2, a3, r1, r2, r3, r4, r5, u1, u2, u3, u4, u5,
    recon, bits, part,
    f0, f1, f2, f3, f4, f5, up, second, third, fourth, grad, sq, rate,
    *, pixels,
):
    fields = (f0, f1, f2, f3, f4, f5)
    place_own((l0, l1, l2, l3, l4, l5), seed[0, 0], fields)
    place_sides(left[...], right[...], fields)
    place_ends(above, below, fields)

    for n in range(BLOCKS):
        up[48 * n : 48 * n + 8, :] = f0[8 + 8 * n : 16 + 8 * n, :]
    for level, ru, cu in ((1, r1, u1), (2, r2, u2), (3, r3, u3), (4, r4, u4), (5, r5, u5)):
        grown = dot(ru[...], jnp.concatenate(split3(fields[level][...]), axis=0))
        full = dot(jnp.concatenate(split3(grown), axis=0), cu[...])
        full = (full[0:80] + full[80:160]) + full[160:240]
        for n in range(BLOCKS):
            up[48 * n + 8 * level : 48 * n + 8 * level + 8, :] = full[8 * n : 8 * n + 8]

    end = EDGE + BLOCK * BLOCKS
    for buf in (second, third, fourth):
        buf[0:EDGE, :] = jnp.zeros((EDGE, LANES), BF16)
        buf[end : end + EDGE, :] = jnp.zeros((EDGE, LANES), BF16)

    def clear(buf):
        @pl.when(ends[0] == 1)
        def _():
            buf[EDGE : EDGE + 96, :] = jnp.zeros((96, LANES), BF16)

        @pl.when(ends[1] == 1)
        def _():
            buf[end - 96 : end, :] = jnp.zeros((96, LANES), BF16)

    def mix(n, _):
        u = up[pl.ds(pl.multiple_of(48 * n, 16), 48), :].astype(BF16)
        first = jnp.maximum(dot(wm1[...], u), 0.0).astype(BF16)
        out = jnp.maximum(dot(wm2[...], first), 0.0).astype(BF16)
        second[pl.ds(pl.multiple_of(EDGE + BLOCK * n, 32), BLOCK), :] = out
        return 0

    lax.fori_loop(0, BLOCKS, mix, 0)
    clear(second)

    def conv(src, dst, w):
        def body(n, _):
            slab = src[pl.ds(pl.multiple_of(BLOCK * n, 64), SLAB), :]
            y = dot(w[...], slab)
            c = y[BLOCK : 2 * BLOCK] + pltpu.roll(y[0:BLOCK], 1, 1)
            c = c + pltpu.roll(y[2 * BLOCK :], LANES - 1, 1)
            rows = pl.ds(pl.multiple_of(EDGE + BLOCK * n, 32), BLOCK)
            dst[rows, :] = (src[rows, :].astype(F32) + jnp.maximum(c, 0.0)).astype(BF16)
            return 0

        lax.fori_loop(0, BLOCKS, body, 0)
        clear(dst)

    conv(second, third, wc1)
    conv(third, fourth, wc2)

    grad[...] = jnp.zeros(grad.shape, F32)
    sq[...] = jnp.zeros(sq.shape, F32)

    def output(n, _):
        slab = fourth[pl.ds(pl.multiple_of(BLOCK * n + 96, 32), SLAB), :]
        y = dot(wout[...].astype(BF16), slab)
        c = y[24:48] + pltpu.roll(y[0:24], 1, 1) + pltpu.roll(y[48:72], LANES - 1, 1)
        rows = pl.ds(pl.multiple_of(8 * n, 8), 8)
        slopes = []
        for o in range(3):
            value = c[8 * o : 8 * o + 8, 0:W]
            recon[o, rows, :] = value
            error = value - target[o, rows, :]
            sq[...] += error * error
            slopes.append((2.0 * error / pixels).astype(BF16).astype(F32))
        slope = jnp.concatenate(slopes, axis=0)
        slope = jnp.concatenate([slope, jnp.zeros((24, LANES - W), F32)], axis=1)
        moved = jnp.concatenate(
            [pltpu.roll(slope, LANES - 1, 1), slope, pltpu.roll(slope, 1, 1)], axis=0
        ).astype(BF16)
        grad[...] += lax.dot_general(
            moved, slab, (((1,), (1,)), ((), ())), preferred_element_type=F32
        )
        return 0

    lax.fori_loop(0, H // 8, output, 0)

    rates = []
    for level in range(LEVELS):
        field = fields[level]
        cols = max(COLS[level], 128)
        wide = WIDE[level]
        rate[...] = jnp.zeros(rate.shape, F32)

        def cells(n, _, level=level, field=field, cols=cols, wide=wide):
            slab = field[pl.ds(pl.multiple_of(8 * n + 8, 8), 16), :]
            moved = [
                slab[:, 0:cols] if j == 0 else pltpu.roll(slab, (-j) % wide, 1)[:, 0:cols]
                for j in range(-2, 3)
            ]
            hi, lo = split2(jnp.concatenate(moved, axis=0))
            inner = jnp.maximum(dot(a1[...], jnp.concatenate([hi, lo, hi], axis=0)), 0.0)
            hi, lo = split2(inner)
            outer = jnp.maximum(dot(a2[...], jnp.concatenate([hi, lo, hi], axis=0)), 0.0)
            hi, lo = split2(outer)
            raw = dot(a3[...], jnp.concatenate([hi, lo, hi], axis=0))
            sigma = raw[8:16]
            soft = jnp.maximum(sigma, 0.0) + jnp.log(1.0 + jnp.exp(-jnp.abs(sigma)))
            row = lax.broadcasted_iota(I32, (8, cols), 0)
            col = lax.broadcasted_iota(I32, (8, cols), 1)
            anchor = ((row + col + parity[level]) & 1) == 0
            centre = jnp.where(anchor, 0.0, raw[0:8])
            spread = jnp.where(anchor, scale[level], 0.1 + soft)
            own = slab[4:12, 0:cols]
            value = laplace(own, centre, spread)
            if level == 0:
                bits[pl.ds(pl.multiple_of(8 * n, 8), 8), :] = value
            if level > 2:
                value = jnp.where((row < ROWS[level]) & (col < COLS[level]), value, 0.0)
            rate[:, 0:cols] += value
            return 0

        count = max(1, ROWS[level] // 8)
        if count == 1:
            cells(0, 0)
        else:
            lax.fori_loop(0, count, cells, 0)
        rates.append(jnp.sum(rate[...]))

    row = lax.broadcasted_iota(I32, (72, SLAB), 0) & 7
    g = grad[...]
    total = jnp.zeros((72, SLAB), F32)
    for r in range(8):
        total = total + jnp.where(row == r, pltpu.roll(g, (-CH * r) % SLAB, 1), 0.0)
    part[...] = jnp.zeros(part.shape, F32)
    for k in range(9):
        part[k : k + 1, :] = jnp.sum(total[8 * k : 8 * k + 8, 0:128], axis=0, keepdims=True)
    lane = lax.broadcasted_iota(I32, (1, 128), 1)
    line = jnp.where(lane == 0, jnp.sum(sq[...]), 0.0)
    for level in range(LEVELS):
        line = jnp.where(lane == 1 + level, rates[level], line)
    part[9:10, :] = line


def pair_steps(lat, lon):
    def flat(f):
        return [(a * lon + b, f(a, b)[0] * lon + f(a, b)[1]) for a in range(lat) for b in range(lon)]

    steps = []
    if (lat, lon) == (8, 32):
        def ring4(v, odd):
            return v ^ 1 if not odd else ((v + 1) % 4 if v & 1 else (v - 1) % 4)

        def far8(z):
            return {1: 6, 6: 1, 2: 5, 5: 2, 3: 0, 0: 3, 4: 7, 7: 4}[z]

        def y_move(a, b, odd):
            y = ring4((a // 4) * 2 + ((b // 2) & 1), odd)
            return (y // 2) * 4 + a % 4, (b & ~2) | ((y & 1) << 1)

        def z_move(a, b, f):
            return a, f(b // 4) * 4 + b % 4

        steps.append(flat(lambda a, b: (a, b ^ 1)))
        for odd in (False, True):
            steps.append(flat(lambda a, b, odd=odd: ((a & ~3) | ring4(a & 3, odd), b)))
        for odd in (False, True):
            steps.append(flat(lambda a, b, odd=odd: y_move(a, b, odd)))
        steps.append(flat(lambda a, b: z_move(a, b, lambda z: z ^ 1)))
        steps.append(flat(lambda a, b: z_move(a, b, lambda z: (z + 1) % 8 if z & 1 else (z - 1) % 8)))
        steps.append(flat(lambda a, b: z_move(a, b, far8)))
        return steps
    k = 1
    while k < lon:
        steps.append(flat(lambda a, b, k=k: (a, b ^ k)))
        k *= 2
    k = 1
    while k < lat:
        steps.append(flat(lambda a, b, k=k: (a ^ k, b)))
        k *= 2
    return steps


def call(kernel, outs, scratch, specs, *args):
    return pl.pallas_call(
        kernel,
        out_shape=outs,
        in_specs=specs,
        out_specs=jax.tree.map(lambda _: VMEM, outs),
        scratch_shapes=scratch,
        compiler_params=pltpu.CompilerParams(vmem_limit_bytes=60 * 1024 * 1024),
    )(*args)


def local(
    target, latent_0, latent_1, latent_2, latent_3, latent_4, latent_5, tile_seeds,
    anchor_parity, anchor_scale, mix_levels, mix_hidden, conv_first, conv_second,
    conv_output, context_in, context_mid, context_out,
):
    lat, lon = lax.axis_size("lat"), lax.axis_size("lon")
    lats = (latent_0, latent_1, latent_2, latent_3, latent_4, latent_5)
    fields = [pltpu.VMEM((TALL[l], WIDE[l]), F32) for l in range(LEVELS)]
    sds = jax.ShapeDtypeStruct
    to_right, to_left = call(
        sides_kernel, (sds((8, 128), F32),) * 2, fields, [SMEM] + [VMEM] * 6, tile_seeds, *lats
    )
    east = [(i, (i + 1) % lon) for i in range(lon)]
    left = lax.ppermute(to_right, "lon", east)
    right = lax.ppermute(to_left, "lon", [(j, i) for i, j in east])
    up, down = call(
        ends_kernel, (sds((8, LANES), F32),) * 2, fields, [SMEM] + [VMEM] * 8,
        tile_seeds, *lats, left, right,
    )
    south = [(i, i + 1) for i in range(lat - 1)]
    above = lax.ppermute(down, "lat", south)
    below = lax.ppermute(up, "lat", [(j, i) for i, j in south])

    names = ("spread", "gather", "place", "tap", "tap_out", "same", "same_out", "levels", "rowof", "ctx")
    prepared = call(
        weights_kernel,
        (
            sds((BLOCK, 48), BF16), sds((BLOCK, BLOCK), BF16), sds((3 * BLOCK, SLAB), BF16),
            sds((3 * BLOCK, SLAB), BF16), sds((72, SLAB), F32), sds((BLOCK, 240), BF16),
            sds((BLOCK, 3 * BLOCK), BF16), sds((16, 3 * BLOCK), BF16),
        ),
        [],
        [VMEM] * (8 + len(names)),
        mix_levels, mix_hidden, conv_first.transpose(2, 3, 0, 1), conv_second.transpose(2, 3, 0, 1),
        conv_output.transpose(0, 2, 3, 1).reshape(27, CH), context_in, context_mid, context_out,
        *[table(n) for n in names],
    )

    index = lax.axis_index("lat")
    ends = jnp.stack([index == 0, index == lat - 1]).astype(I32)
    pixels = float(3 * H * W * lat * lon)
    feature = pltpu.VMEM((2 * EDGE + BLOCK * BLOCKS, LANES), BF16)
    recon, bits, part = call(
        functools.partial(main_kernel, pixels=pixels),
        (sds((3, H, W), F32), sds((H, W), F32), sds((16, 128), F32)),
        fields
        + [pltpu.VMEM((48 * BLOCKS, LANES), F32), feature, feature, feature]
        + [pltpu.VMEM((72, SLAB), F32), pltpu.VMEM((8, W), F32), pltpu.VMEM((8, W), F32)],
        [SMEM] * 4 + [VMEM] * 29,
        tile_seeds, anchor_parity, anchor_scale, ends, *lats, left, right, above, below, target,
        *prepared, *[table(f"rows{l}") for l in range(1, LEVELS)],
        *[table(f"cols{l}") for l in range(1, LEVELS)],
    )
    for step in pair_steps(lat, lon):
        part = part + lax.ppermute(part, ("lat", "lon"), step)
    sizes = [pixels] + [float(ROWS[l] * COLS[l] * lat * lon) for l in range(LEVELS)]
    loss = part[9, 0:7] / jnp.array(sizes, F32)
    grad = part[0:9, 8:80].reshape(3, 3, 3, CH).transpose(1, 3, 2, 0)
    return recon, bits, loss, grad


def solution(mesh):
    tile = P("lat", "lon")
    return jax.shard_map(
        local,
        mesh=mesh,
        in_specs=(P(None, "lat", "lon"),) + (tile,) * 7 + (P(),) * 10,
        out_specs=(P(None, "lat", "lon"), tile, P(), P()),
        check_vma=False,
    )
```

```python
import functools

import jax
import jax.numpy as jnp
import numpy as np
from jax import lax
from jax.experimental import pallas as pl
from jax.experimental.pallas import tpu as pltpu
from jax.sharding import PartitionSpec as P

F32, BF16, I32 = jnp.float32, jnp.bfloat16, jnp.int32
STEPS = (
    (-1, 0), (1, 0), (0, -1), (0, 1), (-2, -1), (-2, 1),
    (2, -1), (2, 1), (-1, -2), (-1, 2), (1, -2), (1, 2),
)
LEVELS, CH, H, W = 6, 24, 64, 512
ROWS = [H >> l for l in range(LEVELS)]
COLS = [W >> l for l in range(LEVELS)]
HALO = [3, 2, 2, 2, 2, 2]
OFFS = [0, 3, 5, 7, 9, 11]
PACK = 13
WIDE = [640, 384, 256, 128, 128, 128]
TALL = [80, 56, 40, 32, 32, 32]
TOP = 12
UPROWS = [0, 48, 32, 16, 16, 16]
LANES = 640
BLOCKS = 9
BLOCK = 8 * CH
SLAB = 256
GROUPS = BLOCK // 16
UNITS = 11
LAST = [(3, 0), (4, 64), (5, 96)]
EDGE = 32
PLACE = [(0, 0), (3, 0), (3, 384), (5, 0), (5, 128), (5, 256)]
VMEM = pl.BlockSpec(memory_space=pltpu.VMEM)
SMEM = pl.BlockSpec(memory_space=pltpu.SMEM)
HBM = pl.BlockSpec(memory_space=pltpu.HBM)
SCALARS = pl.BlockSpec(memory_space=pltpu.HBM)


def dot(a, b):
    return lax.dot_general(a, b, (((1,), (0,)), ((), ())), preferred_element_type=F32)


def dot_t(a, b):
    return lax.dot_general(a, b, (((1,), (1,)), ((), ())), preferred_element_type=F32)


def wrap32(v):
    return int(np.int64(v).astype(np.int32))


def quantize(lat_ref, seed, level):
    shape = lat_ref.shape
    rows = lax.broadcasted_iota(I32, shape, 0)
    cols = lax.broadcasted_iota(I32, shape, 1)
    h = (seed + wrap32(level * 668265263)) + rows * 374761393 + cols * 1103515245
    h = h ^ lax.shift_right_logical(h, jnp.full(shape, 15, I32))
    h = h * 73244475
    h = h ^ lax.shift_right_logical(h, jnp.full(shape, 13, I32))
    h = h * 73244475
    h = h ^ lax.shift_right_logical(h, jnp.full(shape, 16, I32))
    noise = (h & 16777215).astype(F32) * (1.0 / 16777216.0) - 0.5
    return lat_ref[...] + noise


def place_own(lats, seed, fields):
    for level in range(LEVELS):
        fields[level][...] = jnp.zeros(fields[level].shape, F32)
        fields[level][TOP : TOP + ROWS[level], 0 : COLS[level]] = quantize(
            lats[level], seed, level
        )


def place_sides(left, right, fields):
    for level in range(LEVELS):
        base = (COLS[level] // 128) * 128
        for g in range(max(1, ROWS[level] // 8)):
            tile = side_tile(left, right, level, g)
            rows = pl.ds(TOP + 8 * g, 8)
            if base:
                fields[level][rows, base : base + 128] = tile
            else:
                fields[level][rows, 0:128] = fields[level][rows, 0:128] + tile


def place_ends(above, below, fields):
    for level in range(LEVELS):
        h, (r, c), w = HALO[level], PLACE[level], WIDE[level]
        fields[level][TOP - h : TOP, :] = above[r : r + h, c : c + w]
        end = TOP + ROWS[level]
        fields[level][end : end + h, :] = below[r : r + h, c : c + w]


def settle(copies):
    for copy in copies:
        copy.wait()


def side_tile(left, right, level, g):
    h, c = HALO[level], COLS[level]
    lane = lax.broadcasted_iota(I32, (8, 128), 1)
    start = c % 128
    at = PACK * g + OFFS[level]
    tile = jnp.where(
        (lane >= start) & (lane < start + h), pltpu.roll(right, (start - at) % 128, 1), 0.0
    )
    return jnp.where(lane >= 128 - h, pltpu.roll(left, (128 - h - at) % 128, 1), tile)


def sides_kernel(copies, seed, *refs):
    lats, (to_right, to_left), fields = refs[:6], refs[6:8], refs[8:]
    settle(copies)
    place_own(lats, seed[0, 0], fields)
    lane = lax.broadcasted_iota(I32, (8, 128), 1)
    right = jnp.zeros((8, 128), F32)
    left = jnp.zeros((8, 128), F32)
    for level in range(LEVELS):
        h, c = HALO[level], COLS[level]
        base = max(c - 128, 0)
        for g in range(max(1, ROWS[level] // 8)):
            at = PACK * g + OFFS[level]
            here = (lane >= at) & (lane < at + h)
            rows = pl.ds(TOP + 8 * g, 8)
            last = fields[level][rows, base : base + 128]
            first = fields[level][rows, 0:128]
            right = jnp.where(here, pltpu.roll(last, (at - (c - h - base)) % 128, 1), right)
            left = jnp.where(here, pltpu.roll(first, at % 128, 1), left)
    to_right[...] = right
    to_left[...] = left


def ends_kernel(copies, *refs):
    fields, (left, right), (_, up, down) = refs[:6], refs[6:8], refs[8:]
    up[...] = jnp.zeros(up.shape, F32)
    down[...] = jnp.zeros(down.shape, F32)
    for level in range(LEVELS):
        h, (r, c), own = HALO[level], PLACE[level], COLS[level]
        count = max(1, ROWS[level] // 8)
        base = (own // 128) * 128
        for dst, g, skip in ((up, 0, 0), (down, count - 1, min(8, ROWS[level]) - h)):
            tile = side_tile(left[...], right[...], level, g)
            at = TOP + 8 * g + skip
            if base:
                dst[r : r + h, c : c + base] = fields[level][at : at + h, 0:base]
                dst[r : r + h, c + base : c + base + 128] = tile[skip : skip + h]
            else:
                dst[r : r + h, c : c + 128] = (
                    fields[level][at : at + h, :] + tile[skip : skip + h]
                )


def slab_row(d, c):
    return CH * d + EDGE + c


@functools.lru_cache(None)
def tables():
    t = {}
    spread = np.zeros((BLOCK, CH), np.float32)
    for r in range(8):
        for c in range(CH):
            spread[CH * r + c, c] = 1
    t["spread"] = spread
    t["gather"] = np.ascontiguousarray(spread.T)
    place = np.zeros((CH, SLAB), np.float32)
    tap = np.full((BLOCK, SLAB), 9, np.float32)
    for d in range(-1, 9):
        for c in range(CH):
            place[c, slab_row(d, c)] = 1
            for r in range(8):
                tap[CH * r : CH * r + CH, slab_row(d, c)] = d - r + 1
    t["place"], t["tap"] = place, tap
    t["tap_out"] = np.tile(tap[::CH], (3, 1))
    same = np.zeros((BLOCK, BLOCK), np.float32)
    for r in range(8):
        same[CH * r : CH * r + CH, CH * r : CH * r + CH] = 1
    t["same"] = same
    t["same_out"] = np.tile(same[::CH], (2, 1))
    levels = np.zeros((LEVELS, 8 * LEVELS), np.float32)
    rowof = np.zeros((BLOCK, 8 * LEVELS), np.float32)
    for l in range(LEVELS):
        for r in range(8):
            levels[l, 8 * l + r] = 1
            rowof[CH * r : CH * r + CH, 8 * l + r] = 1
    t["levels"], t["rowof"] = levels, rowof
    ctx = np.zeros((8, len(STEPS), 80), np.float32)
    for r in range(8):
        for k, (i, j) in enumerate(STEPS):
            ctx[r, k, (j + 2) * 16 + (r + i + 4)] = 1
    t["ctx"] = ctx
    for l in range(1, LEVELS):
        s = 1 << l
        up_r = np.zeros((72, UPROWS[l]), np.float32)
        for n in range(72):
            y = n - 4
            m, p = y >> l, ((y & (s - 1)) + 0.5) / s - 0.5
            for e, wgt in ((-1, max(-p, 0)), (0, 1 - abs(p)), (1, max(p, 0))):
                at = TOP - 8 + m + e
                if 0 <= at < UPROWS[l]:
                    up_r[n, at] += wgt
        up_c = np.zeros((WIDE[l], LANES), np.float32)
        for n in range(LANES):
            x = n if n < W + 4 else n - LANES
            if x < -4:
                continue
            m, p = x >> l, ((x & (s - 1)) + 0.5) / s - 0.5
            for e, wgt in ((-1, max(-p, 0)), (0, 1 - abs(p)), (1, max(p, 0))):
                q = m + e
                if -HALO[l] <= q < COLS[l] + HALO[l]:
                    up_c[q % WIDE[l], n] += wgt
        t[f"rows{l}"] = np.concatenate([up_r] * 3, axis=1)
        t[f"cols{l}"] = up_c
    return t


def table(name, dtype=BF16):
    return jnp.asarray(tables()[name], dtype)


def split2(x):
    hi = x.astype(BF16)
    return hi, (x - hi.astype(F32)).astype(BF16)


def split3(x):
    hi = x.astype(BF16)
    rest = x - hi.astype(F32)
    mid = rest.astype(BF16)
    return hi, mid, (rest - mid.astype(F32)).astype(BF16)


def conv_weights_kernel(copies, cf, cs, co, spread, place, tap, tap_out, wc1, wc2, wout):
    settle(copies)
    grow = spread[...]
    taps = tap[...].astype(F32)
    for src, dst in ((cf, wc1), (cs, wc2)):
        for b in range(3):
            total = jnp.zeros((BLOCK, SLAB), F32)
            for a in range(3):
                full = dot(dot(grow, src[a, b]).astype(BF16), place[...])
                total = jnp.where(taps == float(a), full, total)
            total = total.astype(BF16)
            for g in range(GROUPS):
                at = 48 * g + 16 * b
                dst[at : at + 16, :] = total[16 * g : 16 * g + 16]
    taps3 = tap_out[...].astype(F32)[0:8]
    for o in range(3):
        rows = [dot(co[o, a], place[...]) for a in range(3)]
        for b in range(3):
            total = jnp.zeros((8, SLAB), F32)
            for a in range(3):
                line = jnp.broadcast_to(rows[a][b : b + 1], (8, SLAB))
                total = jnp.where(taps3 == float(a), line, total)
            at = 24 * b + 8 * o
            wout[at : at + 8, :] = total


def mix_weights_kernel(
    copies, ml, mh, w1, w2, w3, spread, gather, same, same_out, levels, rowof, ctx,
    token, wm1, wm2, a1, a2, a3,
):
    settle(copies)
    token[...] = jnp.zeros(token.shape, F32)
    grow = spread[...]
    wide = gather[...]

    def diag(w):
        return dot(dot(grow, w).astype(BF16), wide) * same[...].astype(F32)

    wm1[...] = (
        dot(dot_t(grow, ml[...]).astype(BF16), levels[...]) * rowof[...].astype(F32)
    ).astype(BF16)
    wm2[...] = diag(mh[...]).astype(BF16)
    hi, lo = split2(w1[...])
    hi, lo = dot_t(grow, hi).astype(BF16), dot_t(grow, lo).astype(BF16)
    for r in range(8):
        rows = slice(CH * r, CH * r + CH)
        sel = ctx[r]
        h, l = dot(hi[rows], sel).astype(BF16), dot(lo[rows], sel).astype(BF16)
        a1[rows, :] = jnp.concatenate([h, h, l], axis=1)
    hi, lo = split2(w2[...])
    h, l = diag(hi).astype(BF16), diag(lo).astype(BF16)
    a2[...] = jnp.concatenate([h, h, l], axis=1)
    hi, lo = split2(w3[...])
    keep = same_out[...].astype(F32)

    def out(w):
        v = dot(w, wide)
        v = jnp.concatenate(
            [jnp.broadcast_to(v[0:1], (8, BLOCK)), jnp.broadcast_to(v[1:2], (8, BLOCK))], axis=0
        )
        return (v * keep).astype(BF16)

    h, l = out(hi), out(lo)
    a3[...] = jnp.concatenate([h, h, l], axis=1)


def laplace(x, centre, spread):
    y = 1.0 / spread
    off = x - centre
    mag = jnp.abs(off)
    inside = jnp.clip(off, -0.5, 0.5)
    e1 = jnp.exp((inside - 0.5) * y)
    e2 = jnp.exp((-0.5 - inside) * y)
    poly = y * (1 - y * (1 / 2 - y * (1 / 6 - y * (1 / 24 - y * (1 / 120)))))
    tail = jnp.where(y < 0.05, poly, 1.0 - e1 * e2)
    beyond = mag >= 0.5
    arg = jnp.where(beyond, 0.5 * tail, 1.0 - 0.5 * (e1 + e2))
    extra = jnp.where(beyond, (mag - 0.5) * y, 0.0)
    return (extra - jnp.log(arg)) * (1.0 / 0.6931471805599453)


def main_kernel(
    copies, parity, scale, q0, q1, q2, q3, q4, q5, left, right, above, below, target,
    wm1, wm2, wc1, wc2, wout, a1, a2, a3, r1, r2, r3, r4, r5, u1, u2, u3, u4, u5,
    recon_out, bits_out, part,
    recon, bits, sems, f0, f1, f2, f3, f4, f5, up, second, third, taps, hidden1, hidden2, own, anchors, moved, sq,
    *, pixels, lat,
):
    fields = (f0, f1, f2, f3, f4, f5)
    settle(copies[:2])
    for src, dst in zip((q0, q1, q2, q3, q4, q5), fields):
        dst[...] = src[...]
    place_sides(left[...], right[...], fields)
    place_ends(above, below, fields)

    lane = lax.broadcasted_iota(I32, (8, 128), 1)
    row = lax.broadcasted_iota(I32, (8, 128), 0)

    def turn(level, n, j):
        slab = fields[level][8 * n + 8 : 8 * n + 24, :]
        cols, wide = max(COLS[level], 128), WIDE[level]
        return (slab if j == 0 else pltpu.roll(slab, (-j) % wide, 1))[:, 0:cols]

    def small(j):
        deep = lax.broadcasted_iota(I32, (16, 128), 1)
        out = jnp.zeros((16, 128), F32)
        for level, at in LAST:
            turned = fields[level][8:24, :]
            if (at - j) % 128:
                turned = pltpu.roll(turned, (at - j) % 128, 1)
            out = jnp.where((deep >= at) & (deep < at + COLS[level]), turned, out)
        return out

    def unit(u, shifted):
        hi, lo = split2(jnp.concatenate(shifted, axis=0))
        taps[u, 0:80, :] = hi
        taps[u, 80:160, :] = lo
        own[u] = shifted[2][4:12]

    for n in range(8):
        unit(n, [turn(0, n, j) for j in range(-2, 3)])
    for n in range(2):
        unit(8 + n, [
            jnp.concatenate([turn(1, 2 * n, j), turn(1, 2 * n + 1, j)], axis=1)
            for j in range(-2, 3)
        ])
    unit(10, [
        jnp.concatenate([turn(2, 0, j), turn(2, 1, j), small(j), jnp.zeros((16, 128), F32)], axis=1)
        for j in range(-2, 3)
    ])

    def cover(level):
        odd = (row + lane + parity[level]) & 1
        plain = jnp.full((8, 128), scale[level], F32)
        return jnp.where(odd == 0, plain, 0.0)

    mixed = jnp.zeros((8, 128), F32)
    for level, at in LAST:
        mixed = jnp.where((lane >= at) & (lane < at + COLS[level]), cover(level), mixed)
    for u in range(UNITS):
        tiles = [cover(0 if u < 8 else 1)] * 4
        if u == 10:
            tiles = [cover(2), cover(2), mixed, mixed]
        anchors[u] = jnp.concatenate(tiles, axis=1)

    taps[UNITS] = jnp.zeros((160, W), BF16)
    own[UNITS] = jnp.zeros((8, W), F32)
    anchors[UNITS] = jnp.ones((8, W), F32)

    settle(copies[3:])
    for n in range(BLOCKS):
        up[48 * n : 48 * n + 8, :] = f0[8 + 8 * n : 16 + 8 * n, :]
    for level, ru, cu in ((1, r1, u1), (2, r2, u2), (3, r3, u3), (4, r4, u4), (5, r5, u5)):
        count = UPROWS[level]
        grown = dot(jnp.concatenate(split3(fields[level][8 : 8 + count, :]), axis=0), cu[...])
        grown = (grown[0:count] + grown[count : 2 * count]) + grown[2 * count :]
        full = dot(ru[...], jnp.concatenate(split3(grown), axis=0))
        for n in range(BLOCKS):
            up[48 * n + 8 * level : 48 * n + 8 * level + 8, :] = full[8 * n : 8 * n + 8]

    end = EDGE + BLOCK * BLOCKS
    for buf in (second, third):
        buf[0:EDGE, :] = jnp.zeros((EDGE, LANES), BF16)
        buf[end : end + EDGE, :] = jnp.zeros((EDGE, LANES), BF16)
    index = lax.axis_index("lat")

    def clear(buf):
        @pl.when(index == 0)
        def _():
            buf[EDGE : EDGE + 96, :] = jnp.zeros((96, LANES), BF16)

        @pl.when(index == lat - 1)
        def _():
            buf[end - 96 : end, :] = jnp.zeros((96, LANES), BF16)

    def block_rows(n):
        return pl.ds(pl.multiple_of(EDGE + BLOCK * n, 32), BLOCK)

    def mix(n):
        u = up[pl.ds(pl.multiple_of(48 * n, 16), 48), :].astype(BF16)
        first = jnp.maximum(dot(wm1[...], u), 0.0).astype(BF16)
        second[block_rows(n), :] = jnp.maximum(dot(wm2[...], first), 0.0).astype(BF16)

    def conv(src, dst, w, n):
        slab = src[pl.ds(pl.multiple_of(BLOCK * n, 64), SLAB), :]
        y = dot(w[...], slab)
        before = src[block_rows(n), :]
        out = []
        for g in range(GROUPS):
            at = 48 * g
            c = y[at + 16 : at + 32] + pltpu.roll(y[at : at + 16], 1, 1)
            c = c + pltpu.roll(y[at + 32 : at + 48], LANES - 1, 1)
            kept = before[16 * g : 16 * g + 16].astype(F32)
            out.append((kept + jnp.maximum(c, 0.0)).astype(BF16))
        dst[block_rows(n), :] = jnp.concatenate(out, axis=0)

    def layer(src, dst, w, u, k):
        hi, lo = src[u, 0:k, :], src[u, k : 2 * k, :]
        hi, lo = split2(jnp.maximum(dot(w[...], jnp.concatenate([hi, lo, hi], axis=0)), 0.0))
        dst[u, 0:BLOCK, :] = hi
        dst[u, BLOCK : 2 * BLOCK, :] = lo

    def cost(u):
        hi, lo = hidden2[u, 0:BLOCK, :], hidden2[u, BLOCK : 2 * BLOCK, :]
        raw = dot(a3[...], jnp.concatenate([hi, lo, hi], axis=0))
        sigma = raw[8:16]
        soft = jnp.maximum(sigma, 0.0) + jnp.log(1.0 + jnp.exp(-jnp.abs(sigma)))
        plain = anchors[u]
        anchor = plain > 0.0
        centre = jnp.where(anchor, 0.0, raw[0:8])
        own[u] = laplace(own[u], centre, jnp.where(anchor, plain, 0.1 + soft))

    def run(synth, entropy):
        def body(t, _):
            for k in range(4):
                if k < 3:
                    synth(3 * t + k)
                entropy(4 * t + k)
            return 0

        lax.fori_loop(0, 3, body, 0)

    run(mix, lambda u: layer(taps, hidden1, a1, u, 80))
    clear(second)
    run(lambda n: conv(second, third, wc1, n), lambda u: layer(hidden1, hidden2, a2, u, BLOCK))
    clear(third)
    run(lambda n: conv(third, second, wc2, n), cost)
    clear(second)

    for n in range(8):
        bits[8 * n : 8 * n + 8, :] = own[n]
    sq[...] = jnp.zeros(sq.shape, F32)

    def output(n):
        slab = second[pl.ds(pl.multiple_of(BLOCK * n + 96, 32), SLAB), :]
        y = dot(wout[...].astype(BF16), slab)
        c = y[24:48] + pltpu.roll(y[0:24], 1, 1) + pltpu.roll(y[48:72], LANES - 1, 1)
        rows = pl.ds(pl.multiple_of(8 * n, 8), 8)
        slopes = []
        total = jnp.zeros((8, W), F32)
        for o in range(3):
            value = c[8 * o : 8 * o + 8, 0:W]
            recon[o, rows, :] = value
            error = value - target[o, rows, :]
            total = total + error * error
            slopes.append((2.0 * error / pixels).astype(BF16).astype(F32))
        slope = jnp.concatenate(slopes, axis=0)
        slope = jnp.concatenate([slope, jnp.zeros((24, LANES - W), F32)], axis=1)
        moved[n, 0:72, :] = jnp.concatenate(
            [pltpu.roll(slope, LANES - 1, 1), slope, pltpu.roll(slope, 1, 1)], axis=0
        ).astype(BF16)
        return total

    def outputs(t, _):
        total = output(4 * t)
        for k in range(1, 4):
            total = total + output(4 * t + k)
        sq[...] += total
        return 0

    settle(copies[2:3])
    send_bits = pltpu.make_async_copy(bits, bits_out, sems.at[0])
    send_bits.start()
    lax.fori_loop(0, 2, outputs, 0)
    send_recon = pltpu.make_async_copy(recon, recon_out, sems.at[1])
    send_recon.start()
    g = jnp.zeros((72, SLAB), F32)
    for n in range(8):
        g = g + dot_t(moved[n, 0:72, :], second[BLOCK * n + 96 : BLOCK * n + 96 + SLAB, :])

    sums = [jnp.zeros((8, W), F32)] * 2
    for n in range(8):
        sums[0] = sums[0] + own[n]
    sums[1] = own[8] + own[9]
    sums.append(own[10, :, 0:128] + own[10, :, 128:256])
    for level, at in LAST:
        keep = (lane >= at) & (lane < at + COLS[level]) & (row < ROWS[level])
        sums.append(jnp.where(keep, own[10, :, 256:384], 0.0))
    row = lax.broadcasted_iota(I32, (72, SLAB), 0) & 7
    total = jnp.zeros((72, SLAB), F32)
    for r in range(8):
        total = total + jnp.where(row == r, pltpu.roll(g, (-CH * r) % SLAB, 1), 0.0)
    part[...] = jnp.zeros(part.shape, F32)
    for k in range(9):
        part[k : k + 1, :] = jnp.sum(total[8 * k : 8 * k + 8, 0:128], axis=0, keepdims=True)
    lane = lax.broadcasted_iota(I32, (1, 128), 1)
    line = jnp.where(lane == 0, jnp.sum(sq[...]), 0.0)
    for level in range(LEVELS):
        line = jnp.where(lane == 1 + level, jnp.sum(sums[level]), line)
    part[9:10, :] = line
    send_bits.wait()
    send_recon.wait()


def final_kernel(copies, mine, other, loss, grad, *, sizes):
    total = mine[...] + other[...]
    lane = lax.broadcasted_iota(I32, (1, 7), 1)
    size = jnp.full((1, 7), sizes[0], F32)
    for k in range(1, 7):
        size = jnp.where(lane == k, sizes[k], size)
    loss[...] = total[9:10, 0:7] / size
    for a in range(3):
        turned = pltpu.roll(total, 128 - 8 - CH * a, 1)
        for b in range(3):
            for o in range(3):
                k = 3 * b + o
                grad[o, a, b : b + 1, :] = turned[k : k + 1, 0:CH]


def pair_steps(lat, lon):
    def flat(f):
        return [(a * lon + b, f(a, b)[0] * lon + f(a, b)[1]) for a in range(lat) for b in range(lon)]

    steps = []
    if (lat, lon) == (8, 32):
        def ring4(v, odd):
            return v ^ 1 if not odd else ((v + 1) % 4 if v & 1 else (v - 1) % 4)

        def far8(z):
            return {1: 6, 6: 1, 2: 5, 5: 2, 3: 0, 0: 3, 4: 7, 7: 4}[z]

        def y_move(a, b, odd):
            y = ring4((a // 4) * 2 + ((b // 2) & 1), odd)
            return (y // 2) * 4 + a % 4, (b & ~2) | ((y & 1) << 1)

        def z_move(a, b, f):
            return a, f(b // 4) * 4 + b % 4

        steps.append(flat(lambda a, b: (a, b ^ 1)))
        for odd in (False, True):
            steps.append(flat(lambda a, b, odd=odd: ((a & ~3) | ring4(a & 3, odd), b)))
        for odd in (False, True):
            steps.append(flat(lambda a, b, odd=odd: y_move(a, b, odd)))
        steps.append(flat(lambda a, b: z_move(a, b, lambda z: z ^ 1)))
        steps.append(flat(lambda a, b: z_move(a, b, lambda z: (z + 1) % 8 if z & 1 else (z - 1) % 8)))
        steps.append(flat(lambda a, b: z_move(a, b, far8)))
        return steps
    k = 1
    while k < lon:
        steps.append(flat(lambda a, b, k=k: (a, b ^ k)))
        k *= 2
    k = 1
    while k < lat:
        steps.append(flat(lambda a, b, k=k: (a ^ k, b)))
        k *= 2
    return steps


def call(kernel, outs, scratch, specs, mib, *args, out_specs=None):
    held = [i for i, spec in enumerate(specs) if spec is HBM or spec is SCALARS]
    many = len(jax.tree.leaves(outs))

    def body(*refs):
        args_in, rest = list(refs[: len(specs)]), refs[len(specs) :]
        outs_in, work = rest[:many], rest[many:]
        bufs, sems, work = work[: len(held)], work[len(held)], work[len(held) + 1 :]
        copies = []
        for k, i in enumerate(held):
            copy = pltpu.make_async_copy(args_in[i], bufs[k], sems.at[k])
            copy.start()
            copies.append(copy)
            args_in[i] = bufs[k]
        kernel(copies, *args_in, *outs_in, *work)

    args = [
        pltpu.with_memory_space_constraint(a, pltpu.HBM) if spec is HBM or spec is SCALARS else a
        for a, spec in zip(args, specs)
    ]
    space = {i: pltpu.SMEM if specs[i] is SCALARS else pltpu.VMEM for i in held}
    buffers = [space[i](args[i].shape, args[i].dtype) for i in held]
    return pl.pallas_call(
        body,
        out_shape=outs,
        in_specs=specs,
        out_specs=out_specs or jax.tree.map(lambda _: VMEM, outs),
        scratch_shapes=buffers + [pltpu.SemaphoreType.DMA((max(1, len(held)),))] + list(scratch),
        compiler_params=pltpu.CompilerParams(vmem_limit_bytes=mib * 1024 * 1024),
        name=getattr(kernel, "func", kernel).__name__,
    )(*args)


def local(
    target, latent_0, latent_1, latent_2, latent_3, latent_4, latent_5, tile_seeds,
    anchor_parity, anchor_scale, mix_levels, mix_hidden, conv_first, conv_second,
    conv_output, context_in, context_mid, context_out,
):
    lat, lon = lax.axis_size("lat"), lax.axis_size("lon")
    lats = (latent_0, latent_1, latent_2, latent_3, latent_4, latent_5)
    fields = [pltpu.VMEM((TALL[l], WIDE[l]), F32) for l in range(LEVELS)]
    sds = jax.ShapeDtypeStruct
    packs = (sds((8, LANES), F32),) * 2
    whole = tuple(sds((TALL[l], WIDE[l]), F32) for l in range(LEVELS))
    to_right, to_left, *quantized = call(
        sides_kernel, (sds((8, 128), F32),) * 2 + whole, [], [SMEM] + [HBM] * 6, 4,
        tile_seeds, *lats,
    )
    east = [(i, (i + 1) % lon) for i in range(lon)]
    left = lax.ppermute(to_right, "lon", east)
    right = lax.ppermute(to_left, "lon", [(j, i) for i, j in east])
    names = ("spread", "gather", "same", "same_out", "levels", "rowof", "ctx")
    token, wm1, wm2, a1, a2, a3 = call(
        mix_weights_kernel,
        (
            sds((8, 128), F32), sds((BLOCK, 48), BF16), sds((BLOCK, BLOCK), BF16),
            sds((BLOCK, 240), BF16), sds((BLOCK, 3 * BLOCK), BF16), sds((16, 3 * BLOCK), BF16),
        ),
        [], [HBM] * (5 + len(names)), 8,
        mix_levels.T, mix_hidden, context_in.T, context_mid, context_out, *[table(n) for n in names],
    )
    up, down = call(
        ends_kernel, packs, [], [VMEM] * 9, 4, *quantized, left, right, token,
    )
    south = [(i, i + 1) for i in range(lat - 1)]
    above = lax.ppermute(down, "lat", south)
    below = lax.ppermute(up, "lat", [(j, i) for i, j in south])
    names = ("spread", "place", "tap", "tap_out")
    wc1, wc2, wout = call(
        conv_weights_kernel,
        (sds((3 * BLOCK, SLAB), BF16), sds((3 * BLOCK, SLAB), BF16), sds((72, SLAB), F32)),
        [], [HBM] * (3 + len(names)), 8,
        conv_first.transpose(2, 3, 0, 1), conv_second.transpose(2, 3, 0, 1),
        conv_output.transpose(0, 2, 3, 1), *[table(n) for n in names],
    )

    pixels = float(3 * H * W * lat * lon)
    feature = pltpu.VMEM((2 * EDGE + BLOCK * BLOCKS, LANES), BF16)
    hidden = pltpu.VMEM((UNITS + 1, 2 * BLOCK, W), BF16)
    plain = pltpu.VMEM((UNITS + 1, 8, W), F32)
    fields = [pltpu.VMEM((TALL[l], WIDE[l]), F32) for l in range(LEVELS)]
    recon, bits, part = call(
        functools.partial(main_kernel, pixels=pixels, lat=lat),
        (sds((3, H, W), F32), sds((H, W), F32), sds((16, 128), F32)),
        [pltpu.VMEM((3, H, W), F32), pltpu.VMEM((H, W), F32), pltpu.SemaphoreType.DMA((2,))]
        + fields
        + [pltpu.VMEM((48 * BLOCKS, LANES), F32), feature, feature]
        + [pltpu.VMEM((UNITS + 1, 160, W), BF16), hidden, hidden, plain, plain]
        + [pltpu.VMEM((8, 80, LANES), BF16), pltpu.VMEM((8, W), F32)],
        [SCALARS] * 2 + [VMEM] * 10 + [HBM] + [VMEM] * 8 + [HBM] * 10,
        32,
        anchor_parity, anchor_scale, *quantized, left, right, above, below, target,
        wm1, wm2, wc1, wc2, wout, a1, a2, a3,
        *[table(f"rows{l}") for l in range(1, LEVELS)],
        *[table(f"cols{l}") for l in range(1, LEVELS)],
        out_specs=(HBM, HBM, VMEM),
    )
    steps = pair_steps(lat, lon)
    for step in steps[:-1]:
        part = part + lax.ppermute(part, ("lat", "lon"), step)
    other = lax.ppermute(part, ("lat", "lon"), steps[-1])
    sizes = [pixels] + [float(ROWS[l] * COLS[l] * lat * lon) for l in range(LEVELS)]
    loss, grad = call(
        functools.partial(final_kernel, sizes=sizes),
        (sds((1, 7), F32), sds((3, 3, 3, CH), F32)), [], [VMEM] * 2, 1, part, other,
    )
    return recon, bits, loss.reshape(7), grad.transpose(0, 3, 1, 2)


def solution(mesh):
    tile = P("lat", "lon")
    return jax.shard_map(
        local,
        mesh=mesh,
        in_specs=(P(None, "lat", "lon"),) + (tile,) * 7 + (P(),) * 10,
        out_specs=(P(None, "lat", "lon"), tile, P(), P()),
        check_vma=False,
    )
```

```python
import functools

import jax
import jax.numpy as jnp
import numpy as np
from jax import lax
from jax.experimental import pallas as pl
from jax.experimental.pallas import tpu as pltpu
from jax.sharding import PartitionSpec as P

F32, BF16, I32 = jnp.float32, jnp.bfloat16, jnp.int32
STEPS = (
    (-1, 0), (1, 0), (0, -1), (0, 1), (-2, -1), (-2, 1),
    (2, -1), (2, 1), (-1, -2), (-1, 2), (1, -2), (1, 2),
)
LEVELS, CH, H, W = 6, 24, 64, 512
ROWS = [H >> l for l in range(LEVELS)]
COLS = [W >> l for l in range(LEVELS)]
HALO = [3, 2, 2, 2, 2, 2]
OFFS = [0, 3, 5, 7, 9, 11]
PACK = 13
WIDE = [640, 384, 256, 128, 128, 128]
TALL = [80, 56, 40, 32, 32, 32]
TOP = 12
UPROWS = [0, 48, 32, 16, 16, 16]
LANES = 640
BLOCKS = 9
BLOCK = 8 * CH
SLAB = 256
HALF = 4 * CH
PAIR = 2 * CH
SHORT = 160
UNITS = 11
LAST = [(3, 0), (4, 64), (5, 96)]
EDGE = 32
PLACE = [(0, 0), (3, 0), (3, 384), (5, 0), (5, 128), (5, 256)]
VMEM = pl.BlockSpec(memory_space=pltpu.VMEM)
SMEM = pl.BlockSpec(memory_space=pltpu.SMEM)
HBM = pl.BlockSpec(memory_space=pltpu.HBM)
SCALARS = pl.BlockSpec(memory_space=pltpu.HBM)


def dot(a, b):
    return lax.dot_general(a, b, (((1,), (0,)), ((), ())), preferred_element_type=F32)


def dot_t(a, b):
    return lax.dot_general(a, b, (((1,), (1,)), ((), ())), preferred_element_type=F32)


def wrap32(v):
    return int(np.int64(v).astype(np.int32))


def quantize(lat_ref, seed, level):
    shape = lat_ref.shape
    rows = lax.broadcasted_iota(I32, shape, 0)
    cols = lax.broadcasted_iota(I32, shape, 1)
    h = (seed + wrap32(level * 668265263)) + rows * 374761393 + cols * 1103515245
    h = h ^ lax.shift_right_logical(h, jnp.full(shape, 15, I32))
    h = h * 73244475
    h = h ^ lax.shift_right_logical(h, jnp.full(shape, 13, I32))
    h = h * 73244475
    h = h ^ lax.shift_right_logical(h, jnp.full(shape, 16, I32))
    noise = (h & 16777215).astype(F32) * (1.0 / 16777216.0) - 0.5
    return lat_ref[...] + noise


def place_own(lats, seed, fields):
    for level in range(LEVELS):
        fields[level][...] = jnp.zeros(fields[level].shape, F32)
        fields[level][TOP : TOP + ROWS[level], 0 : COLS[level]] = quantize(
            lats[level], seed, level
        )


def place_sides(left, right, fields):
    for level in range(LEVELS):
        base = (COLS[level] // 128) * 128
        for g in range(max(1, ROWS[level] // 8)):
            tile = side_tile(left, right, level, g)
            rows = pl.ds(TOP + 8 * g, 8)
            if base:
                fields[level][rows, base : base + 128] = tile
            else:
                fields[level][rows, 0:128] = fields[level][rows, 0:128] + tile


def place_ends(above, below, fields):
    for level in range(LEVELS):
        h, (r, c), w = HALO[level], PLACE[level], WIDE[level]
        fields[level][TOP - h : TOP, :] = above[r : r + h, c : c + w]
        end = TOP + ROWS[level]
        fields[level][end : end + h, :] = below[r : r + h, c : c + w]


def settle(copies):
    for copy in copies:
        copy.wait()


def side_tile(left, right, level, g):
    h, c = HALO[level], COLS[level]
    lane = lax.broadcasted_iota(I32, (8, 128), 1)
    start = c % 128
    at = PACK * g + OFFS[level]
    tile = jnp.where(
        (lane >= start) & (lane < start + h), pltpu.roll(right, (start - at) % 128, 1), 0.0
    )
    return jnp.where(lane >= 128 - h, pltpu.roll(left, (128 - h - at) % 128, 1), tile)


def sides_kernel(copies, seed, *refs):
    lats, (to_right, to_left), fields = refs[:6], refs[6:8], refs[8:]
    settle(copies)
    place_own(lats, seed[0, 0], fields)
    lane = lax.broadcasted_iota(I32, (8, 128), 1)
    right = jnp.zeros((8, 128), F32)
    left = jnp.zeros((8, 128), F32)
    for level in range(LEVELS):
        h, c = HALO[level], COLS[level]
        base = max(c - 128, 0)
        for g in range(max(1, ROWS[level] // 8)):
            at = PACK * g + OFFS[level]
            here = (lane >= at) & (lane < at + h)
            rows = pl.ds(TOP + 8 * g, 8)
            last = fields[level][rows, base : base + 128]
            first = fields[level][rows, 0:128]
            right = jnp.where(here, pltpu.roll(last, (at - (c - h - base)) % 128, 1), right)
            left = jnp.where(here, pltpu.roll(first, at % 128, 1), left)
    to_right[...] = right
    to_left[...] = left


def ends_kernel(copies, *refs):
    fields, (left, right), (_, up, down) = refs[:6], refs[6:8], refs[8:]
    up[...] = jnp.zeros(up.shape, F32)
    down[...] = jnp.zeros(down.shape, F32)
    for level in range(LEVELS):
        h, (r, c), own = HALO[level], PLACE[level], COLS[level]
        count = max(1, ROWS[level] // 8)
        base = (own // 128) * 128
        for dst, g, skip in ((up, 0, 0), (down, count - 1, min(8, ROWS[level]) - h)):
            tile = side_tile(left[...], right[...], level, g)
            at = TOP + 8 * g + skip
            if base:
                dst[r : r + h, c : c + base] = fields[level][at : at + h, 0:base]
                dst[r : r + h, c + base : c + base + 128] = tile[skip : skip + h]
            else:
                dst[r : r + h, c : c + 128] = (
                    fields[level][at : at + h, :] + tile[skip : skip + h]
                )


def slab_row(d, c):
    return CH * d + EDGE + c


@functools.lru_cache(None)
def tables():
    t = {}
    spread = np.zeros((BLOCK, CH), np.float32)
    for r in range(8):
        for c in range(CH):
            spread[CH * r + c, c] = 1
    t["spread"] = spread
    t["gather"] = np.ascontiguousarray(spread.T)
    place = np.zeros((CH, SLAB), np.float32)
    tap = np.full((BLOCK, SLAB), 9, np.float32)
    for d in range(-1, 9):
        for c in range(CH):
            place[c, slab_row(d, c)] = 1
            for r in range(8):
                tap[CH * r : CH * r + CH, slab_row(d, c)] = d - r + 1
    t["place"], t["tap"] = place, tap
    t["tap_out"] = np.tile(tap[::CH], (3, 1))
    same = np.zeros((BLOCK, BLOCK), np.float32)
    for r in range(8):
        same[CH * r : CH * r + CH, CH * r : CH * r + CH] = 1
    t["same"] = same
    t["same_out"] = np.tile(same[::CH], (2, 1))
    levels = np.zeros((LEVELS, 8 * LEVELS), np.float32)
    rowof = np.zeros((BLOCK, 8 * LEVELS), np.float32)
    for l in range(LEVELS):
        for r in range(8):
            levels[l, 8 * l + r] = 1
            rowof[CH * r : CH * r + CH, 8 * l + r] = 1
    t["levels"], t["rowof"] = levels, rowof
    ctx = np.zeros((8, len(STEPS), 80), np.float32)
    for r in range(8):
        for k, (i, j) in enumerate(STEPS):
            ctx[r, k, (j + 2) * 16 + (r + i + 4)] = 1
    t["ctx"] = ctx
    return t


def table(name, dtype=BF16):
    return jnp.asarray(tables()[name], dtype)


def split2(x):
    hi = x.astype(BF16)
    return hi, (x - hi.astype(F32)).astype(BF16)


def split3(x):
    hi = x.astype(BF16)
    rest = x - hi.astype(F32)
    mid = rest.astype(BF16)
    return hi, mid, (rest - mid.astype(F32)).astype(BF16)


def hat(shape, level, fine, coarse):
    place = (fine + 0.5) * (1.0 / (1 << level)) - 0.5
    return jnp.maximum(1.0 - jnp.abs(place - coarse), 0.0).astype(BF16)


def conv_weights_kernel(
    copies, cf, cs, co, spread, place, tap, tap_out, wc1, wc2, wout, *scales
):
    row_scales, col_scales = scales[:5], scales[5:]
    for level in range(1, LEVELS):
        count = UPROWS[level]
        shape = (72, 3 * count)
        fine = lax.broadcasted_iota(I32, shape, 0) - 4
        at = lax.broadcasted_iota(I32, shape, 1)
        at = jnp.where(at >= 2 * count, at - 2 * count, jnp.where(at >= count, at - count, at))
        row_scales[level - 1][...] = hat(
            shape, level, fine.astype(F32), (at + (8 - TOP)).astype(F32)
        )
        own, wide, h = COLS[level], WIDE[level], HALO[level]
        for first in range(0, wide, 128):
            shape = (128, LANES)
            fine = lax.broadcasted_iota(I32, shape, 1)
            fine = jnp.where(fine < W + 4, fine, jnp.where(fine >= LANES - 4, fine - LANES, -99999))
            at = lax.broadcasted_iota(I32, shape, 0) + first
            at = jnp.where(at < own + h, at, jnp.where(at >= wide - h, at - wide, 99999))
            col_scales[level - 1][first : first + 128, :] = hat(
                shape, level, fine.astype(F32), at.astype(F32)
            )
    settle(copies)
    grow = spread[0:HALF, :]
    short = place[:, 0:SHORT]
    taps = tap[0:HALF, 0:SHORT].astype(F32)
    for src, dst in ((cf, wc1), (cs, wc2)):
        for b in range(3):
            total = jnp.zeros((HALF, SHORT), F32)
            for a in range(3):
                full = dot(dot(grow, src[a, b]).astype(BF16), short)
                total = jnp.where(taps == float(a), full, total)
            dst[:, SHORT * b : SHORT * b + SHORT] = total.astype(BF16)
    taps3 = tap_out[...].astype(F32)[0:8]
    for o in range(3):
        rows = [dot(co[o, a], place[...]) for a in range(3)]
        for b in range(3):
            total = jnp.zeros((8, SLAB), F32)
            for a in range(3):
                line = jnp.broadcast_to(rows[a][b : b + 1], (8, SLAB))
                total = jnp.where(taps3 == float(a), line, total)
            at = 24 * b + 8 * o
            wout[at : at + 8, :] = total


def mix_weights_kernel(
    copies, ml, mh, w1, w2, w3, spread, gather, same, same_out, levels, rowof, ctx,
    token, wm1, wm2, a1, a2, a3,
):
    settle(copies)
    token[...] = jnp.zeros(token.shape, F32)
    grow = spread[...]
    wide = gather[...]

    def diag(w):
        return dot(dot(grow, w).astype(BF16), wide) * same[...].astype(F32)

    wm1[...] = (
        dot(dot_t(grow, ml[...]).astype(BF16), levels[...]) * rowof[...].astype(F32)
    ).astype(BF16)
    wm2[...] = diag(mh[...]).astype(BF16)
    hi, lo = split2(w1[...])
    hi, lo = dot_t(grow, hi).astype(BF16), dot_t(grow, lo).astype(BF16)
    for r in range(8):
        rows = slice(CH * r, CH * r + CH)
        sel = ctx[r]
        h, l = dot(hi[rows], sel).astype(BF16), dot(lo[rows], sel).astype(BF16)
        a1[rows, :] = jnp.concatenate([h, h, l], axis=1)
    hi, lo = split2(w2[...])
    h, l = diag(hi).astype(BF16)[0:PAIR, 0:PAIR], diag(lo).astype(BF16)[0:PAIR, 0:PAIR]
    a2[...] = jnp.concatenate([h, h, l], axis=1)
    hi, lo = split2(w3[...])
    keep = same_out[...].astype(F32)

    def out(w):
        v = dot(w, wide)
        v = jnp.concatenate(
            [jnp.broadcast_to(v[0:1], (8, BLOCK)), jnp.broadcast_to(v[1:2], (8, BLOCK))], axis=0
        )
        return (v * keep).astype(BF16)

    h, l = out(hi), out(lo)
    a3[...] = jnp.concatenate([h, h, l], axis=1)


def laplace(x, centre, spread):
    y = 1.0 / spread
    off = x - centre
    mag = jnp.abs(off)
    inside = jnp.clip(off, -0.5, 0.5)
    e1 = jnp.exp((inside - 0.5) * y)
    e2 = jnp.exp((-0.5 - inside) * y)
    poly = y * (1 - y * (1 / 2 - y * (1 / 6 - y * (1 / 24 - y * (1 / 120)))))
    tail = jnp.where(y < 0.05, poly, 1.0 - e1 * e2)
    beyond = mag >= 0.5
    arg = jnp.where(beyond, 0.5 * tail, 1.0 - 0.5 * (e1 + e2))
    extra = jnp.where(beyond, (mag - 0.5) * y, 0.0)
    return (extra - jnp.log(arg)) * (1.0 / 0.6931471805599453)


def main_kernel(
    copies, parity, scale, q0, q1, q2, q3, q4, q5, left, right, above, below, target,
    wm1, wm2, wc1, wc2, wout, a1, a2, a3, r1, r2, r3, r4, r5, u1, u2, u3, u4, u5,
    recon_out, bits_out, part,
    recon, bits, sems, f0, f1, f2, f3, f4, f5, up, second, third, taps, hidden1, hidden2, own, anchors, moved, sq,
    *, pixels, lat,
):
    fields = (f0, f1, f2, f3, f4, f5)
    for src, dst in zip((q0, q1, q2, q3, q4, q5), fields):
        dst[...] = src[...]
    place_sides(left[...], right[...], fields)
    place_ends(above, below, fields)

    for n in range(BLOCKS):
        up[48 * n : 48 * n + 8, :] = f0[8 + 8 * n : 16 + 8 * n, :]
    for level, ru, cu in ((1, r1, u1), (2, r2, u2), (3, r3, u3), (4, r4, u4), (5, r5, u5)):
        count = UPROWS[level]
        grown = dot(jnp.concatenate(split3(fields[level][8 : 8 + count, :]), axis=0), cu[...])
        grown = (grown[0:count] + grown[count : 2 * count]) + grown[2 * count :]
        full = dot(ru[...], jnp.concatenate(split3(grown), axis=0))
        for n in range(BLOCKS):
            up[48 * n + 8 * level : 48 * n + 8 * level + 8, :] = full[8 * n : 8 * n + 8]

    lane = lax.broadcasted_iota(I32, (8, 128), 1)
    row = lax.broadcasted_iota(I32, (8, 128), 0)

    turned = {}
    for level in range(3):
        for j in range(-2, 3):
            rows = fields[level][8 : 24 + ROWS[level] - 8, :]
            turned[level, j] = pltpu.roll(rows, (-j) % WIDE[level], 1) if j else rows

    def turn(level, n, j):
        return turned[level, j][8 * n : 8 * n + 16, 0 : max(COLS[level], 128)]

    def small(j):
        deep = lax.broadcasted_iota(I32, (16, 128), 1)
        out = jnp.zeros((16, 128), F32)
        for level, at in LAST:
            turned = fields[level][8:24, :]
            if (at - j) % 128:
                turned = pltpu.roll(turned, (at - j) % 128, 1)
            out = jnp.where((deep >= at) & (deep < at + COLS[level]), turned, out)
        return out

    def unit(u, shifted):
        hi, lo = split2(jnp.concatenate(shifted, axis=0))
        taps[u, 0:80, :] = hi
        taps[u, 80:160, :] = lo
        own[u] = shifted[2][4:12]

    for n in range(8):
        unit(n, [turn(0, n, j) for j in range(-2, 3)])
    for n in range(2):
        unit(8 + n, [
            jnp.concatenate([turn(1, 2 * n, j), turn(1, 2 * n + 1, j)], axis=1)
            for j in range(-2, 3)
        ])
    unit(10, [
        jnp.concatenate([turn(2, 0, j), turn(2, 1, j), small(j), jnp.zeros((16, 128), F32)], axis=1)
        for j in range(-2, 3)
    ])

    settle(copies[:2])

    def cover(level):
        odd = (row + lane + parity[level]) & 1
        plain = jnp.full((8, 128), scale[level], F32)
        return jnp.where(odd == 0, plain, 0.0)

    mixed = jnp.zeros((8, 128), F32)
    for level, at in LAST:
        mixed = jnp.where((lane >= at) & (lane < at + COLS[level]), cover(level), mixed)
    for u in range(UNITS):
        tiles = [cover(0 if u < 8 else 1)] * 4
        if u == 10:
            tiles = [cover(2), cover(2), mixed, mixed]
        anchors[u] = jnp.concatenate(tiles, axis=1)

    taps[UNITS] = jnp.zeros((160, W), BF16)
    own[UNITS] = jnp.zeros((8, W), F32)
    anchors[UNITS] = jnp.ones((8, W), F32)

    end = EDGE + BLOCK * BLOCKS
    for buf in (second, third):
        buf[:, 0:EDGE, :] = jnp.zeros((3, EDGE, LANES), BF16)
        buf[:, end : end + EDGE, :] = jnp.zeros((3, EDGE, LANES), BF16)
    index = lax.axis_index("lat")

    def clear(buf):
        @pl.when(index == 0)
        def _():
            buf[:, EDGE : EDGE + 96, :] = jnp.zeros((3, 96, LANES), BF16)

        @pl.when(index == lat - 1)
        def _():
            buf[:, end - 96 : end, :] = jnp.zeros((3, 96, LANES), BF16)

    def block_rows(n):
        return pl.ds(EDGE + BLOCK * n, BLOCK)

    def mix(n):
        u = up[pl.ds(48 * n, 48), :].astype(BF16)
        first = jnp.maximum(dot(wm1[...], u), 0.0).astype(BF16)
        value = jnp.maximum(dot(wm2[...], first), 0.0).astype(BF16)
        put(second, block_rows(n), value)

    def put(buf, rows, value):
        buf[1, rows, :] = value
        buf[0, rows, :] = pltpu.roll(value, 1, 1)
        buf[2, rows, :] = pltpu.roll(value, LANES - 1, 1)

    def conv(src, w, n, part):
        slab = pl.ds(BLOCK * n + HALF * part, SHORT)
        rows = pl.ds(EDGE + BLOCK * n + HALF * part, HALF)
        c = dot(w[...], jnp.concatenate([src[b, slab, :] for b in range(3)], axis=0))
        return rows, (src[1, rows, :].astype(F32) + jnp.maximum(c, 0.0)).astype(BF16)

    def conv_one(n):
        for part in range(2):
            rows, value = conv(second, wc1, n, part)
            put(third, rows, value)

    def conv_two(n):
        for part in range(2):
            rows, value = conv(third, wc2, n, part)
            second[1, rows, :] = value

    def middle(u):
        for k in range(4):
            hi = hidden1[u, PAIR * k : PAIR * k + PAIR, :]
            lo = hidden1[u, BLOCK + PAIR * k : BLOCK + PAIR * k + PAIR, :]
            out = jnp.maximum(dot(a2[...], jnp.concatenate([hi, lo, hi], axis=0)), 0.0)
            hi, lo = split2(out)
            hidden2[u, PAIR * k : PAIR * k + PAIR, :] = hi
            hidden2[u, BLOCK + PAIR * k : BLOCK + PAIR * k + PAIR, :] = lo

    def layer(src, dst, w, u, k):
        hi, lo = src[u, 0:k, :], src[u, k : 2 * k, :]
        hi, lo = split2(jnp.maximum(dot(w[...], jnp.concatenate([hi, lo, hi], axis=0)), 0.0))
        dst[u, 0:BLOCK, :] = hi
        dst[u, BLOCK : 2 * BLOCK, :] = lo

    def cost(u):
        hi, lo = hidden2[u, 0:BLOCK, :], hidden2[u, BLOCK : 2 * BLOCK, :]
        raw = dot(a3[...], jnp.concatenate([hi, lo, hi], axis=0))
        sigma = raw[8:16]
        soft = jnp.maximum(sigma, 0.0) + jnp.log(1.0 + jnp.exp(-jnp.abs(sigma)))
        plain = anchors[u]
        anchor = plain > 0.0
        centre = jnp.where(anchor, 0.0, raw[0:8])
        own[u] = laplace(own[u], centre, jnp.where(anchor, plain, 0.1 + soft))

    def run(synth, entropy):
        def body(t, _):
            for k in range(4):
                if k < 3:
                    synth(3 * t + k)
                if 4 * t + k < UNITS:
                    entropy(4 * t + k)
            return 0

        for t in range(3):
            body(t, 0)

    run(mix, lambda u: layer(taps, hidden1, a1, u, 80))
    clear(second)
    run(conv_one, middle)
    clear(third)
    run(conv_two, cost)
    clear(second)

    for n in range(8):
        bits[8 * n : 8 * n + 8, :] = own[n]

    def output(n):
        slab = second[1, BLOCK * n + 96 : BLOCK * n + 96 + SLAB, :]
        y = dot(wout[...].astype(BF16), slab)
        c = y[24:48] + pltpu.roll(y[0:24], 1, 1) + pltpu.roll(y[48:72], LANES - 1, 1)
        rows = slice(8 * n, 8 * n + 8)
        slopes = []
        total = jnp.zeros((8, W), F32)
        for o in range(3):
            value = c[8 * o : 8 * o + 8, 0:W]
            recon[o, rows, :] = value
            error = value - target[o, rows, :]
            total = total + error * error
            slopes.append((2.0 * error / pixels).astype(BF16).astype(F32))
        slope = jnp.concatenate(slopes, axis=0)
        slope = jnp.concatenate([slope, jnp.zeros((24, LANES - W), F32)], axis=1)
        moved[n, 0:72, :] = jnp.concatenate(
            [pltpu.roll(slope, LANES - 1, 1), slope, pltpu.roll(slope, 1, 1)], axis=0
        ).astype(BF16)
        return total

    settle(copies[2:3])
    send_bits = pltpu.make_async_copy(bits, bits_out, sems.at[0])
    send_bits.start()
    total = jnp.zeros((8, W), F32)
    g = jnp.zeros((72, SLAB), F32)
    for n in range(8):
        total = total + output(n)
    for n in range(8):
        g = g + dot_t(moved[n, 0:72, :], second[1, BLOCK * n + 96 : BLOCK * n + 96 + SLAB, :])
    sq[...] = total
    send_recon = pltpu.make_async_copy(recon, recon_out, sems.at[1])
    send_recon.start()
    sums = [jnp.zeros((8, W), F32)] * 2
    for n in range(8):
        sums[0] = sums[0] + own[n]
    sums[1] = own[8] + own[9]
    sums.append(own[10, :, 0:128] + own[10, :, 128:256])
    for level, at in LAST:
        keep = (lane >= at) & (lane < at + COLS[level]) & (row < ROWS[level])
        sums.append(jnp.where(keep, own[10, :, 256:384], 0.0))
    row = lax.broadcasted_iota(I32, (72, SLAB), 0) & 7
    total = jnp.zeros((72, SLAB), F32)
    for r in range(8):
        total = total + jnp.where(row == r, pltpu.roll(g, (-CH * r) % SLAB, 1), 0.0)
    part[...] = jnp.zeros(part.shape, F32)
    for k in range(9):
        part[k : k + 1, :] = jnp.sum(total[8 * k : 8 * k + 8, 0:128], axis=0, keepdims=True)
    lane = lax.broadcasted_iota(I32, (1, 128), 1)
    line = jnp.where(lane == 0, jnp.sum(sq[...]), 0.0)
    for level in range(LEVELS):
        line = jnp.where(lane == 1 + level, jnp.sum(sums[level]), line)
    part[9:10, :] = line
    send_bits.wait()
    send_recon.wait()


def final_kernel(copies, mine, other, loss, grad, *, sizes):
    total = mine[...] + other[...]
    lane = lax.broadcasted_iota(I32, (1, 7), 1)
    size = jnp.full((1, 7), sizes[0], F32)
    for k in range(1, 7):
        size = jnp.where(lane == k, sizes[k], size)
    loss[...] = total[9:10, 0:7] / size
    for a in range(3):
        turned = pltpu.roll(total, 128 - 8 - CH * a, 1)
        for b in range(3):
            for o in range(3):
                k = 3 * b + o
                grad[o, a, b : b + 1, :] = turned[k : k + 1, 0:CH]


def pair_steps(lat, lon):
    def flat(f):
        return [(a * lon + b, f(a, b)[0] * lon + f(a, b)[1]) for a in range(lat) for b in range(lon)]

    steps = []
    if (lat, lon) == (8, 32):
        def ring4(v, odd):
            return v ^ 1 if not odd else ((v + 1) % 4 if v & 1 else (v - 1) % 4)

        def far8(z):
            return {1: 6, 6: 1, 2: 5, 5: 2, 3: 0, 0: 3, 4: 7, 7: 4}[z]

        def y_move(a, b, odd):
            y = ring4((a // 4) * 2 + ((b // 2) & 1), odd)
            return (y // 2) * 4 + a % 4, (b & ~2) | ((y & 1) << 1)

        def z_move(a, b, f):
            return a, f(b // 4) * 4 + b % 4

        steps.append(flat(lambda a, b: (a, b ^ 1)))
        for odd in (False, True):
            steps.append(flat(lambda a, b, odd=odd: ((a & ~3) | ring4(a & 3, odd), b)))
        for odd in (False, True):
            steps.append(flat(lambda a, b, odd=odd: y_move(a, b, odd)))
        steps.append(flat(lambda a, b: z_move(a, b, lambda z: z ^ 1)))
        steps.append(flat(lambda a, b: z_move(a, b, lambda z: (z + 1) % 8 if z & 1 else (z - 1) % 8)))
        steps.append(flat(lambda a, b: z_move(a, b, far8)))
        return steps
    k = 1
    while k < lon:
        steps.append(flat(lambda a, b, k=k: (a, b ^ k)))
        k *= 2
    k = 1
    while k < lat:
        steps.append(flat(lambda a, b, k=k: (a ^ k, b)))
        k *= 2
    return steps


def call(kernel, outs, scratch, specs, mib, *args, out_specs=None):
    held = [i for i, spec in enumerate(specs) if spec is HBM or spec is SCALARS]
    many = len(jax.tree.leaves(outs))

    def body(*refs):
        args_in, rest = list(refs[: len(specs)]), refs[len(specs) :]
        outs_in, work = rest[:many], rest[many:]
        bufs, sems, work = work[: len(held)], work[len(held)], work[len(held) + 1 :]
        copies = []
        for k, i in enumerate(held):
            copy = pltpu.make_async_copy(args_in[i], bufs[k], sems.at[k])
            copy.start()
            copies.append(copy)
            args_in[i] = bufs[k]
        kernel(copies, *args_in, *outs_in, *work)

    args = [
        pltpu.with_memory_space_constraint(a, pltpu.HBM) if spec is HBM or spec is SCALARS else a
        for a, spec in zip(args, specs)
    ]
    space = {i: pltpu.SMEM if specs[i] is SCALARS else pltpu.VMEM for i in held}
    buffers = [space[i](args[i].shape, args[i].dtype) for i in held]
    return pl.pallas_call(
        body,
        out_shape=outs,
        in_specs=specs,
        out_specs=out_specs or jax.tree.map(lambda _: VMEM, outs),
        scratch_shapes=buffers + [pltpu.SemaphoreType.DMA((max(1, len(held)),))] + list(scratch),
        compiler_params=pltpu.CompilerParams(vmem_limit_bytes=mib * 1024 * 1024),
        name=getattr(kernel, "func", kernel).__name__,
    )(*args)


def local(
    target, latent_0, latent_1, latent_2, latent_3, latent_4, latent_5, tile_seeds,
    anchor_parity, anchor_scale, mix_levels, mix_hidden, conv_first, conv_second,
    conv_output, context_in, context_mid, context_out,
):
    lat, lon = lax.axis_size("lat"), lax.axis_size("lon")
    lats = (latent_0, latent_1, latent_2, latent_3, latent_4, latent_5)
    fields = [pltpu.VMEM((TALL[l], WIDE[l]), F32) for l in range(LEVELS)]
    sds = jax.ShapeDtypeStruct
    packs = (sds((8, LANES), F32),) * 2
    whole = tuple(sds((TALL[l], WIDE[l]), F32) for l in range(LEVELS))
    to_right, to_left, *quantized = call(
        sides_kernel, (sds((8, 128), F32),) * 2 + whole, [], [SMEM] + [HBM] * 6, 4,
        tile_seeds, *lats,
    )
    east = [(i, (i + 1) % lon) for i in range(lon)]
    left = lax.ppermute(to_right, "lon", east)
    right = lax.ppermute(to_left, "lon", [(j, i) for i, j in east])
    names = ("spread", "gather", "same", "same_out", "levels", "rowof", "ctx")
    token, wm1, wm2, a1, a2, a3 = call(
        mix_weights_kernel,
        (
            sds((8, 128), F32), sds((BLOCK, 48), BF16), sds((BLOCK, BLOCK), BF16),
            sds((BLOCK, 240), BF16), sds((PAIR, 3 * PAIR), BF16), sds((16, 3 * BLOCK), BF16),
        ),
        [], [HBM] * (5 + len(names)), 8,
        mix_levels.T, mix_hidden, context_in.T, context_mid, context_out, *[table(n) for n in names],
    )
    up, down = call(
        ends_kernel, packs, [], [VMEM] * 9, 4, *quantized, left, right, token,
    )
    south = [(i, i + 1) for i in range(lat - 1)]
    above = lax.ppermute(down, "lat", south)
    below = lax.ppermute(up, "lat", [(j, i) for i, j in south])
    names = ("spread", "place", "tap", "tap_out")
    wc1, wc2, wout, *scales = call(
        conv_weights_kernel,
        (sds((HALF, 3 * SHORT), BF16), sds((HALF, 3 * SHORT), BF16), sds((72, SLAB), F32))
        + tuple(sds((72, 3 * UPROWS[l]), BF16) for l in range(1, LEVELS))
        + tuple(sds((WIDE[l], LANES), BF16) for l in range(1, LEVELS)),
        [], [HBM] * (3 + len(names)), 8,
        conv_first.transpose(2, 3, 0, 1), conv_second.transpose(2, 3, 0, 1),
        conv_output.transpose(0, 2, 3, 1), *[table(n) for n in names],
    )

    pixels = float(3 * H * W * lat * lon)
    feature = pltpu.VMEM((3, 2 * EDGE + BLOCK * BLOCKS, LANES), BF16)
    hidden = pltpu.VMEM((UNITS + 1, 2 * BLOCK, W), BF16)
    plain = pltpu.VMEM((UNITS + 1, 8, W), F32)
    fields = [pltpu.VMEM((TALL[l], WIDE[l]), F32) for l in range(LEVELS)]
    recon, bits, part = call(
        functools.partial(main_kernel, pixels=pixels, lat=lat),
        (sds((3, H, W), F32), sds((H, W), F32), sds((16, 128), F32)),
        [pltpu.VMEM((3, H, W), F32), pltpu.VMEM((H, W), F32), pltpu.SemaphoreType.DMA((2,))]
        + fields
        + [pltpu.VMEM((48 * BLOCKS, LANES), F32), feature, feature]
        + [pltpu.VMEM((UNITS + 1, 160, W), BF16), hidden, hidden, plain, plain]
        + [pltpu.VMEM((8, 80, LANES), BF16), pltpu.VMEM((8, W), F32)],
        [SCALARS] * 2 + [VMEM] * 10 + [HBM] + [VMEM] * 18,
        40,
        anchor_parity, anchor_scale, *quantized, left, right, above, below, target,
        wm1, wm2, wc1, wc2, wout, a1, a2, a3,
        *scales,
        out_specs=(HBM, HBM, VMEM),
    )
    steps = pair_steps(lat, lon)
    for step in steps[:-1]:
        part = part + lax.ppermute(part, ("lat", "lon"), step)
    other = lax.ppermute(part, ("lat", "lon"), steps[-1])
    sizes = [pixels] + [float(ROWS[l] * COLS[l] * lat * lon) for l in range(LEVELS)]
    loss, grad = call(
        functools.partial(final_kernel, sizes=sizes),
        (sds((1, 7), F32), sds((3, 3, 3, CH), F32)), [], [VMEM] * 2, 1, part, other,
    )
    return recon, bits, loss.reshape(7), grad.transpose(0, 3, 1, 2)


def solution(mesh):
    tile = P("lat", "lon")
    return jax.shard_map(
        local,
        mesh=mesh,
        in_specs=(P(None, "lat", "lon"),) + (tile,) * 7 + (P(),) * 10,
        out_specs=(P(None, "lat", "lon"), tile, P(), P()),
        check_vma=False,
    )
```

```python
import functools

import jax
import jax.numpy as jnp
import numpy as np
from jax import lax
from jax.experimental import pallas as pl
from jax.experimental.pallas import tpu as pltpu
from jax.sharding import PartitionSpec as P


F32, BF16, I32 = jnp.float32, jnp.bfloat16, jnp.int32
STEPS = (
    (-1, 0), (1, 0), (0, -1), (0, 1), (-2, -1), (-2, 1),
    (2, -1), (2, 1), (-1, -2), (-1, 2), (1, -2), (1, 2),
)
LEVELS, CH, H, W = 6, 24, 64, 512
ROWS = [H >> l for l in range(LEVELS)]
COLS = [W >> l for l in range(LEVELS)]
HALO = [3, 2, 2, 2, 2, 2]
OFFS = [0, 3, 5, 7, 9, 11]
PACK = 13
WIDE = [640, 384, 256, 128, 128, 128]
TALL = [80, 56, 40, 32, 32, 32]
TOP = 12
UPROWS = [0, 48, 32, 16, 16, 16]
LANES = 640
BLOCKS = 9
BLOCK = 8 * CH
SLAB = 256
HALF = 4 * CH
PAIR = 2 * CH
SHORT = 160
UNITS = 11
LAST = [(3, 0), (4, 64), (5, 96)]
EDGE = 32
PLACE = [(0, 0), (3, 0), (3, 384), (5, 0), (5, 128), (5, 256)]
VMEM = pl.BlockSpec(memory_space=pltpu.VMEM)
SMEM = pl.BlockSpec(memory_space=pltpu.SMEM)
HBM = pl.BlockSpec(memory_space=pltpu.HBM)
SCALARS = pl.BlockSpec(memory_space=pltpu.HBM)


def dot(a, b):
    return lax.dot_general(a, b, (((1,), (0,)), ((), ())), preferred_element_type=F32)


def dot_t(a, b):
    return lax.dot_general(a, b, (((1,), (1,)), ((), ())), preferred_element_type=F32)


def wrap32(v):
    return int(np.int64(v).astype(np.int32))


def quantize(lat_ref, seed, level):
    shape = lat_ref.shape
    rows = lax.broadcasted_iota(I32, shape, 0)
    cols = lax.broadcasted_iota(I32, shape, 1)
    h = (seed + wrap32(level * 668265263)) + rows * 374761393 + cols * 1103515245
    h = h ^ lax.shift_right_logical(h, jnp.full(shape, 15, I32))
    h = h * 73244475
    h = h ^ lax.shift_right_logical(h, jnp.full(shape, 13, I32))
    h = h * 73244475
    h = h ^ lax.shift_right_logical(h, jnp.full(shape, 16, I32))
    noise = (h & 16777215).astype(F32) * (1.0 / 16777216.0) - 0.5
    return lat_ref[...] + noise


def place_own(lats, seed, fields):
    for level in range(LEVELS):
        fields[level][...] = jnp.zeros(fields[level].shape, F32)
        fields[level][TOP : TOP + ROWS[level], 0 : COLS[level]] = quantize(
            lats[level], seed, level
        )


def place_sides(left, right, fields):
    for level in range(LEVELS):
        base = (COLS[level] // 128) * 128
        for g in range(max(1, ROWS[level] // 8)):
            tile = side_tile(left, right, level, g)
            rows = pl.ds(TOP + 8 * g, 8)
            if base:
                fields[level][rows, base : base + 128] = tile
            else:
                fields[level][rows, 0:128] = fields[level][rows, 0:128] + tile


def place_ends(above, below, fields):
    for level in range(LEVELS):
        h, (r, c), w = HALO[level], PLACE[level], WIDE[level]
        fields[level][TOP - h : TOP, :] = above[r : r + h, c : c + w]
        end = TOP + ROWS[level]
        fields[level][end : end + h, :] = below[r : r + h, c : c + w]


def settle(copies):
    for copy in copies:
        copy.wait()


def side_tile(left, right, level, g):
    h, c = HALO[level], COLS[level]
    lane = lax.broadcasted_iota(I32, (8, 128), 1)
    start = c % 128
    at = PACK * g + OFFS[level]
    tile = jnp.where(
        (lane >= start) & (lane < start + h), pltpu.roll(right, (start - at) % 128, 1), 0.0
    )
    return jnp.where(lane >= 128 - h, pltpu.roll(left, (128 - h - at) % 128, 1), tile)


def hat(level, fine, coarse):
    place = (fine + 0.5) * (1.0 / (1 << level)) - 0.5
    return jnp.maximum(1.0 - jnp.abs(place - coarse), 0.0).astype(BF16)


def sides_kernel(copies, seed, *refs):
    lats, (near, far), fields, scales = refs[:6], refs[6:8], refs[8:14], refs[14:]
    row_scales, col_scales = scales[:5], scales[5:]
    for level in range(1, LEVELS):
        count = UPROWS[level]
        shape = (72, 3 * count)
        fine = lax.broadcasted_iota(I32, shape, 0) - 4
        at = lax.broadcasted_iota(I32, shape, 1)
        at = jnp.where(at >= 2 * count, at - 2 * count, jnp.where(at >= count, at - count, at))
        row_scales[level - 1][...] = hat(level, fine.astype(F32), (at + (8 - TOP)).astype(F32))
        own, wide, h = COLS[level], WIDE[level], HALO[level]
        for first in range(0, wide, 128):
            shape = (128, LANES)
            fine = lax.broadcasted_iota(I32, shape, 1)
            fine = jnp.where(fine < W + 4, fine, jnp.where(fine >= LANES - 4, fine - LANES, -99999))
            at = lax.broadcasted_iota(I32, shape, 0) + first
            at = jnp.where(at < own + h, at, jnp.where(at >= wide - h, at - wide, 99999))
            col_scales[level - 1][first : first + 128, :] = hat(
                level, fine.astype(F32), at.astype(F32)
            )
    settle(copies[:6])
    place_own(lats, seed[0, 0], fields)
    lane = lax.broadcasted_iota(I32, (8, 128), 1)
    right = jnp.zeros((8, 128), F32)
    left = jnp.zeros((8, 128), F32)
    for level in range(LEVELS):
        h, c = HALO[level], COLS[level]
        base = max(c - 128, 0)
        for g in range(max(1, ROWS[level] // 8)):
            at = PACK * g + OFFS[level]
            here = (lane >= at) & (lane < at + h)
            rows = pl.ds(TOP + 8 * g, 8)
            last = fields[level][rows, base : base + 128]
            first = fields[level][rows, 0:128]
            right = jnp.where(here, pltpu.roll(last, (at - (c - h - base)) % 128, 1), right)
            left = jnp.where(here, pltpu.roll(first, at % 128, 1), left)
    odd = (lax.axis_index("lon") & 1) == 1
    near[...] = jnp.where(odd, left, right)
    far[...] = jnp.where(odd, right, left)
    settle(copies[6:])


def ordered(axis, near, far):
    odd = (lax.axis_index(axis) & 1) == 1
    return jnp.where(odd, near[...], far[...]), jnp.where(odd, far[...], near[...])


def ends_kernel(copies, *refs):
    fields, sides, (_, near_out, far_out, up, down) = refs[:6], refs[6:8], refs[8:]
    left, right = ordered("lon", *sides)
    up[...] = jnp.zeros(up.shape, F32)
    down[...] = jnp.zeros(down.shape, F32)
    for level in range(LEVELS):
        h, (r, c), own = HALO[level], PLACE[level], COLS[level]
        count = max(1, ROWS[level] // 8)
        base = (own // 128) * 128
        for dst, g, skip in ((up, 0, 0), (down, count - 1, min(8, ROWS[level]) - h)):
            tile = side_tile(left, right, level, g)
            at = TOP + 8 * g + skip
            if base:
                dst[r : r + h, c : c + base] = fields[level][at : at + h, 0:base]
                dst[r : r + h, c + base : c + base + 128] = tile[skip : skip + h]
            else:
                dst[r : r + h, c : c + 128] = (
                    fields[level][at : at + h, :] + tile[skip : skip + h]
                )
    odd = (lax.axis_index("lat") & 1) == 1
    near_out[...] = jnp.where(odd, up[...], down[...])
    far_out[...] = jnp.where(odd, down[...], up[...])


def slab_row(d, c):
    return CH * d + EDGE + c


@functools.lru_cache(None)
def tables():
    t = {}
    spread = np.zeros((BLOCK, CH), np.float32)
    for r in range(8):
        for c in range(CH):
            spread[CH * r + c, c] = 1
    t["spread"] = spread
    t["gather"] = np.ascontiguousarray(spread.T)
    place = np.zeros((CH, SLAB), np.float32)
    tap = np.full((BLOCK, SLAB), 9, np.float32)
    for d in range(-1, 9):
        for c in range(CH):
            place[c, slab_row(d, c)] = 1
            for r in range(8):
                tap[CH * r : CH * r + CH, slab_row(d, c)] = d - r + 1
    t["place"], t["tap"] = place, tap
    t["tap_out"] = np.tile(tap[::CH], (3, 1))
    same = np.zeros((BLOCK, BLOCK), np.float32)
    for r in range(8):
        same[CH * r : CH * r + CH, CH * r : CH * r + CH] = 1
    t["same"] = same
    t["same_out"] = np.tile(same[::CH], (2, 1))
    levels = np.zeros((LEVELS, 8 * LEVELS), np.float32)
    rowof = np.zeros((BLOCK, 8 * LEVELS), np.float32)
    for l in range(LEVELS):
        for r in range(8):
            levels[l, 8 * l + r] = 1
            rowof[CH * r : CH * r + CH, 8 * l + r] = 1
    t["levels"], t["rowof"] = levels, rowof
    ctx = np.zeros((8, len(STEPS), 80), np.float32)
    for r in range(8):
        for k, (i, j) in enumerate(STEPS):
            ctx[r, k, (j + 2) * 16 + (r + i + 4)] = 1
    t["ctx"] = ctx
    return t


def table(name, dtype=BF16):
    return jnp.asarray(tables()[name], dtype)


def split2(x):
    hi = x.astype(BF16)
    return hi, (x - hi.astype(F32)).astype(BF16)


def split3(x):
    hi = x.astype(BF16)
    rest = x - hi.astype(F32)
    mid = rest.astype(BF16)
    return hi, mid, (rest - mid.astype(F32)).astype(BF16)


def conv_weights_kernel(
    copies, cf, cs, co, spread, place, tap, tap_out, wc1, wc2, wout
):
    settle(copies)
    grow = spread[0:HALF, :]
    short = place[:, 0:SHORT]
    taps = tap[0:HALF, 0:SHORT].astype(F32)
    for src, dst in ((cf, wc1), (cs, wc2)):
        for b in range(3):
            total = jnp.zeros((HALF, SHORT), F32)
            for a in range(3):
                full = dot(dot(grow, src[a, b]).astype(BF16), short)
                total = jnp.where(taps == float(a), full, total)
            dst[:, SHORT * b : SHORT * b + SHORT] = total.astype(BF16)
    taps3 = tap_out[...].astype(F32)[0:8]
    for o in range(3):
        rows = [dot(co[o, a], place[...]) for a in range(3)]
        for b in range(3):
            total = jnp.zeros((8, SLAB), F32)
            for a in range(3):
                line = jnp.broadcast_to(rows[a][b : b + 1], (8, SLAB))
                total = jnp.where(taps3 == float(a), line, total)
            at = 24 * b + 8 * o
            wout[at : at + 8, :] = total


def mix_weights_kernel(
    copies, ml, mh, w1, w2, w3, spread, gather, same, same_out, levels, rowof, ctx,
    token, wm1, wm2, a1, a2, a3,
):
    settle(copies)
    token[...] = jnp.zeros(token.shape, F32)
    grow = spread[...]
    wide = gather[...]

    def diag(w):
        return dot(dot(grow, w).astype(BF16), wide) * same[...].astype(F32)

    wm1[...] = (
        dot(dot_t(grow, ml[...]).astype(BF16), levels[...]) * rowof[...].astype(F32)
    ).astype(BF16)
    wm2[...] = diag(mh[...]).astype(BF16)
    hi, lo = split2(w1[...])
    hi, lo = dot_t(grow, hi).astype(BF16), dot_t(grow, lo).astype(BF16)
    for r in range(8):
        rows = slice(CH * r, CH * r + CH)
        sel = ctx[r]
        h, l = dot(hi[rows], sel).astype(BF16), dot(lo[rows], sel).astype(BF16)
        a1[rows, :] = jnp.concatenate([h, h, l], axis=1)
    hi, lo = split2(w2[...])
    h, l = diag(hi).astype(BF16)[0:PAIR, 0:PAIR], diag(lo).astype(BF16)[0:PAIR, 0:PAIR]
    a2[...] = jnp.concatenate([h, h, l], axis=1)
    hi, lo = split2(w3[...])
    keep = same_out[...].astype(F32)

    def out(w):
        v = dot(w, wide)
        v = jnp.concatenate(
            [jnp.broadcast_to(v[0:1], (8, BLOCK)), jnp.broadcast_to(v[1:2], (8, BLOCK))], axis=0
        )
        return (v * keep).astype(BF16)

    h, l = out(hi), out(lo)
    a3[...] = jnp.concatenate([h, h, l], axis=1)


def laplace(x, centre, spread):
    y = 1.0 / spread
    off = x - centre
    mag = jnp.abs(off)
    inside = jnp.clip(off, -0.5, 0.5)
    e1 = jnp.exp((inside - 0.5) * y)
    e2 = jnp.exp((-0.5 - inside) * y)
    poly = y * (1 - y * (1 / 2 - y * (1 / 6 - y * (1 / 24 - y * (1 / 120)))))
    tail = jnp.where(y < 0.05, poly, 1.0 - e1 * e2)
    beyond = mag >= 0.5
    arg = jnp.where(beyond, 0.5 * tail, 1.0 - 0.5 * (e1 + e2))
    extra = jnp.where(beyond, (mag - 0.5) * y, 0.0)
    return (extra - jnp.log(arg)) * (1.0 / 0.6931471805599453)


def main_kernel(
    copies, parity, scale, q0, q1, q2, q3, q4, q5, side_near, side_far, end_near, end_far, target,
    wm1, wm2, wc1, wc2, wout, a1, a2, a3, r1, r2, r3, r4, r5, u1, u2, u3, u4, u5,
    recon_out, bits_out, part,
    recon, bits, sems, f0, f1, f2, f3, f4, f5, up, second, third, taps, hidden1, hidden2, own, anchors, moved, sq,
    *, pixels, lat,
):
    fields = (f0, f1, f2, f3, f4, f5)
    for src, dst in zip((q0, q1, q2, q3, q4, q5), fields):
        dst[...] = src[...]
    place_sides(*ordered("lon", side_near, side_far), fields)
    place_ends(*ordered("lat", end_near, end_far), fields)

    for n in range(BLOCKS):
        up[48 * n : 48 * n + 8, :] = f0[8 + 8 * n : 16 + 8 * n, :]
    for level, ru, cu in ((1, r1, u1), (2, r2, u2), (3, r3, u3), (4, r4, u4), (5, r5, u5)):
        count = UPROWS[level]
        grown = dot(jnp.concatenate(split3(fields[level][8 : 8 + count, :]), axis=0), cu[...])
        grown = (grown[0:count] + grown[count : 2 * count]) + grown[2 * count :]
        full = dot(ru[...], jnp.concatenate(split3(grown), axis=0))
        for n in range(BLOCKS):
            up[48 * n + 8 * level : 48 * n + 8 * level + 8, :] = full[8 * n : 8 * n + 8]

    lane = lax.broadcasted_iota(I32, (8, 128), 1)
    row = lax.broadcasted_iota(I32, (8, 128), 0)

    turned = {}
    for level in range(3):
        for j in range(-2, 3):
            rows = fields[level][8 : 24 + ROWS[level] - 8, :]
            turned[level, j] = pltpu.roll(rows, (-j) % WIDE[level], 1) if j else rows

    def turn(level, n, j):
        return turned[level, j][8 * n : 8 * n + 16, 0 : max(COLS[level], 128)]

    def small(j):
        deep = lax.broadcasted_iota(I32, (16, 128), 1)
        out = jnp.zeros((16, 128), F32)
        for level, at in LAST:
            turned = fields[level][8:24, :]
            if (at - j) % 128:
                turned = pltpu.roll(turned, (at - j) % 128, 1)
            out = jnp.where((deep >= at) & (deep < at + COLS[level]), turned, out)
        return out

    def unit(u, shifted):
        hi, lo = split2(jnp.concatenate(shifted, axis=0))
        taps[u, 0:80, :] = hi
        taps[u, 80:160, :] = lo
        own[u] = shifted[2][4:12]

    for n in range(8):
        unit(n, [turn(0, n, j) for j in range(-2, 3)])
    for n in range(2):
        unit(8 + n, [
            jnp.concatenate([turn(1, 2 * n, j), turn(1, 2 * n + 1, j)], axis=1)
            for j in range(-2, 3)
        ])
    unit(10, [
        jnp.concatenate([turn(2, 0, j), turn(2, 1, j), small(j), jnp.zeros((16, 128), F32)], axis=1)
        for j in range(-2, 3)
    ])

    settle(copies[:2])

    def cover(level):
        odd = (row + lane + parity[level]) & 1
        plain = jnp.full((8, 128), scale[level], F32)
        return jnp.where(odd == 0, plain, 0.0)

    mixed = jnp.zeros((8, 128), F32)
    for level, at in LAST:
        mixed = jnp.where((lane >= at) & (lane < at + COLS[level]), cover(level), mixed)
    for u in range(UNITS):
        tiles = [cover(0 if u < 8 else 1)] * 4
        if u == 10:
            tiles = [cover(2), cover(2), mixed, mixed]
        anchors[u] = jnp.concatenate(tiles, axis=1)

    taps[UNITS] = jnp.zeros((160, W), BF16)
    own[UNITS] = jnp.zeros((8, W), F32)
    anchors[UNITS] = jnp.ones((8, W), F32)

    end = EDGE + BLOCK * BLOCKS
    for buf in (second, third):
        buf[:, 0:EDGE, :] = jnp.zeros((3, EDGE, LANES), BF16)
        buf[:, end : end + EDGE, :] = jnp.zeros((3, EDGE, LANES), BF16)
    index = lax.axis_index("lat")

    def clear(buf):
        @pl.when(index == 0)
        def _():
            buf[:, EDGE : EDGE + 96, :] = jnp.zeros((3, 96, LANES), BF16)

        @pl.when(index == lat - 1)
        def _():
            buf[:, end - 96 : end, :] = jnp.zeros((3, 96, LANES), BF16)

    def block_rows(n):
        return pl.ds(EDGE + BLOCK * n, BLOCK)

    def mix(n):
        u = up[pl.ds(48 * n, 48), :].astype(BF16)
        first = jnp.maximum(dot(wm1[...], u), 0.0).astype(BF16)
        value = jnp.maximum(dot(wm2[...], first), 0.0).astype(BF16)
        put(second, block_rows(n), value)

    def put(buf, rows, value):
        buf[1, rows, :] = value
        buf[0, rows, :] = pltpu.roll(value, 1, 1)
        buf[2, rows, :] = pltpu.roll(value, LANES - 1, 1)

    def conv(src, w, n):
        taps_of = []
        for part in range(2):
            at = BLOCK * n + HALF * part
            taps_of.append([src[b, at : at + SHORT, :] for b in range(3)])
        main = [dot(w[...], jnp.concatenate([t[:, 0:W] for t in taps], axis=0)) for taps in taps_of]
        edge = dot(
            w[...],
            jnp.concatenate(
                [
                    jnp.concatenate([taps_of[0][b][:, W:], taps_of[1][b][:, W:]], axis=1)
                    for b in range(3)
                ],
                axis=0,
            ),
        )
        out = []
        for part in range(2):
            at = EDGE + BLOCK * n + HALF * part
            rows = pl.ds(at, HALF)
            tail = edge[:, (LANES - W) * part : (LANES - W) * (part + 1)]
            c = jnp.concatenate([main[part], tail], axis=1)
            out.append((rows, (src[1, rows, :].astype(F32) + jnp.maximum(c, 0.0)).astype(BF16)))
        return out

    def conv_one(n):
        for rows, value in conv(second, wc1, n):
            put(third, rows, value)

    def conv_two(n):
        for rows, value in conv(third, wc2, n):
            second[1, rows, :] = value

    def middle(u):
        for k in range(4):
            hi = hidden1[u, PAIR * k : PAIR * k + PAIR, :]
            lo = hidden1[u, BLOCK + PAIR * k : BLOCK + PAIR * k + PAIR, :]
            out = jnp.maximum(dot(a2[...], jnp.concatenate([hi, lo, hi], axis=0)), 0.0)
            hi, lo = split2(out)
            hidden2[u, PAIR * k : PAIR * k + PAIR, :] = hi
            hidden2[u, BLOCK + PAIR * k : BLOCK + PAIR * k + PAIR, :] = lo

    def layer(src, dst, w, u, k):
        hi, lo = src[u, 0:k, :], src[u, k : 2 * k, :]
        hi, lo = split2(jnp.maximum(dot(w[...], jnp.concatenate([hi, lo, hi], axis=0)), 0.0))
        dst[u, 0:BLOCK, :] = hi
        dst[u, BLOCK : 2 * BLOCK, :] = lo

    def cost(u):
        hi, lo = hidden2[u, 0:BLOCK, :], hidden2[u, BLOCK : 2 * BLOCK, :]
        raw = dot(a3[...], jnp.concatenate([hi, lo, hi], axis=0))
        sigma = raw[8:16]
        soft = jnp.maximum(sigma, 0.0) + jnp.log(1.0 + jnp.exp(-jnp.abs(sigma)))
        plain = anchors[u]
        anchor = plain > 0.0
        centre = jnp.where(anchor, 0.0, raw[0:8])
        own[u] = laplace(own[u], centre, jnp.where(anchor, plain, 0.1 + soft))

    def run(synth, entropy):
        def body(t):
            for k in range(4):
                if k < 3:
                    synth(3 * t + k)
                if 4 * t + k < UNITS:
                    entropy(4 * t + k)
            return 0

        for t in range(3):
            body(t)

    run(mix, lambda u: layer(taps, hidden1, a1, u, 80))
    clear(second)
    run(conv_one, middle)
    clear(third)
    run(conv_two, cost)
    clear(second)

    for n in range(8):
        bits[8 * n : 8 * n + 8, :] = own[n]

    def output(n):
        slab = second[1, BLOCK * n + 96 : BLOCK * n + 96 + SLAB, :]
        y = dot(wout[...].astype(BF16), slab)
        c = y[24:48] + pltpu.roll(y[0:24], 1, 1) + pltpu.roll(y[48:72], LANES - 1, 1)
        rows = slice(8 * n, 8 * n + 8)
        slopes = []
        total = jnp.zeros((8, W), F32)
        for o in range(3):
            value = c[8 * o : 8 * o + 8, 0:W]
            recon[o, rows, :] = value
            error = value - target[o, rows, :]
            total = total + error * error
            slopes.append((2.0 * error / pixels).astype(BF16).astype(F32))
        slope = jnp.concatenate(slopes, axis=0)
        slope = jnp.concatenate([slope, jnp.zeros((24, LANES - W), F32)], axis=1)
        moved[n, 0:72, :] = jnp.concatenate(
            [pltpu.roll(slope, LANES - 1, 1), slope, pltpu.roll(slope, 1, 1)], axis=0
        ).astype(BF16)
        return total

    settle(copies[2:3])
    send_bits = pltpu.make_async_copy(bits, bits_out, sems.at[0])
    send_bits.start()
    total = jnp.zeros((8, W), F32)
    g = jnp.zeros((72, SLAB), F32)
    for n in range(8):
        total = total + output(n)
    for n in range(8):
        g = g + dot_t(moved[n, 0:72, :], second[1, BLOCK * n + 96 : BLOCK * n + 96 + SLAB, :])
    sq[...] = total
    send_recon = pltpu.make_async_copy(recon, recon_out, sems.at[1])
    send_recon.start()
    sums = [jnp.zeros((8, W), F32)] * 2
    for n in range(8):
        sums[0] = sums[0] + own[n]
    sums[1] = own[8] + own[9]
    sums.append(own[10, :, 0:128] + own[10, :, 128:256])
    for level, at in LAST:
        keep = (lane >= at) & (lane < at + COLS[level]) & (row < ROWS[level])
        sums.append(jnp.where(keep, own[10, :, 256:384], 0.0))
    row = lax.broadcasted_iota(I32, (72, SLAB), 0) & 7
    total = jnp.zeros((72, SLAB), F32)
    for r in range(8):
        total = total + jnp.where(row == r, pltpu.roll(g, (-CH * r) % SLAB, 1), 0.0)
    part[...] = jnp.zeros(part.shape, F32)
    for k in range(9):
        part[k : k + 1, :] = jnp.sum(total[8 * k : 8 * k + 8, 0:128], axis=0, keepdims=True)
    lane = lax.broadcasted_iota(I32, (1, 128), 1)
    line = jnp.where(lane == 0, jnp.sum(sq[...]), 0.0)
    for level in range(LEVELS):
        line = jnp.where(lane == 1 + level, jnp.sum(sums[level]), line)
    part[9:10, :] = line
    send_bits.wait()
    send_recon.wait()


def final_kernel(copies, mine, other, loss, grad, *, sizes):
    total = mine[...] + other[...]
    lane = lax.broadcasted_iota(I32, (1, 7), 1)
    size = jnp.full((1, 7), sizes[0], F32)
    for k in range(1, 7):
        size = jnp.where(lane == k, sizes[k], size)
    loss[...] = total[9:10, 0:7] / size
    for a in range(3):
        turned = pltpu.roll(total, 128 - 8 - CH * a, 1)
        for b in range(3):
            for o in range(3):
                k = 3 * b + o
                grad[o, a, b : b + 1, :] = turned[k : k + 1, 0:CH]


def pair_steps(lat, lon):
    def flat(f):
        return [(a * lon + b, f(a, b)[0] * lon + f(a, b)[1]) for a in range(lat) for b in range(lon)]

    steps = []
    if (lat, lon) == (8, 32):
        def ring4(v, odd):
            return v ^ 1 if not odd else ((v + 1) % 4 if v & 1 else (v - 1) % 4)

        def far8(z):
            return {1: 6, 6: 1, 2: 5, 5: 2, 3: 0, 0: 3, 4: 7, 7: 4}[z]

        def y_move(a, b, odd):
            y = ring4((a // 4) * 2 + ((b // 2) & 1), odd)
            return (y // 2) * 4 + a % 4, (b & ~2) | ((y & 1) << 1)

        def z_move(a, b, f):
            return a, f(b // 4) * 4 + b % 4

        steps.append(flat(lambda a, b: (a, b ^ 1)))
        for odd in (False, True):
            steps.append(flat(lambda a, b, odd=odd: ((a & ~3) | ring4(a & 3, odd), b)))
        for odd in (False, True):
            steps.append(flat(lambda a, b, odd=odd: y_move(a, b, odd)))
        steps.append(flat(lambda a, b: z_move(a, b, lambda z: z ^ 1)))
        steps.append(flat(lambda a, b: z_move(a, b, lambda z: (z + 1) % 8 if z & 1 else (z - 1) % 8)))
        steps.append(flat(lambda a, b: z_move(a, b, far8)))
        return steps
    k = 1
    while k < lon:
        steps.append(flat(lambda a, b, k=k: (a, b ^ k)))
        k *= 2
    k = 1
    while k < lat:
        steps.append(flat(lambda a, b, k=k: (a ^ k, b)))
        k *= 2
    return steps


def call(kernel, outs, scratch, specs, mib, *args, out_specs=None, forward=()):
    own = len(args)
    args = args + tuple(forward)
    specs = specs + [HBM] * len(forward)
    outs = outs + tuple(jax.ShapeDtypeStruct(a.shape, a.dtype) for a in forward)
    held = [i for i, spec in enumerate(specs) if spec is HBM or spec is SCALARS]
    many = len(jax.tree.leaves(outs))

    def body(*refs):
        args_in, rest = list(refs[: len(specs)]), refs[len(specs) :]
        outs_in, work = rest[:many], rest[many:]
        bufs, sems, work = work[: inner], work[inner], work[inner + 1 :]
        bufs = list(bufs) + list(outs_in[many - len(forward) :])
        copies = []
        for k, i in enumerate(held):
            copy = pltpu.make_async_copy(args_in[i], bufs[k], sems.at[k])
            copy.start()
            copies.append(copy)
            args_in[i] = bufs[k]
        kernel(copies, *args_in[:own], *outs_in[: many - len(forward)], *work)

    args = [
        pltpu.with_memory_space_constraint(a, pltpu.HBM) if spec is HBM or spec is SCALARS else a
        for a, spec in zip(args, specs)
    ]
    space = {i: pltpu.SMEM if specs[i] is SCALARS else pltpu.VMEM for i in held}
    buffers = [space[i](args[i].shape, args[i].dtype) for i in held if i < own]
    inner = len(buffers)
    return pl.pallas_call(
        body,
        out_shape=outs,
        in_specs=specs,
        out_specs=out_specs or jax.tree.map(lambda _: VMEM, outs),
        scratch_shapes=buffers + [pltpu.SemaphoreType.DMA((max(1, len(held)),))] + list(scratch),
        compiler_params=pltpu.CompilerParams(vmem_limit_bytes=mib * 1024 * 1024),
    )(*args)


def local(
    target, latent_0, latent_1, latent_2, latent_3, latent_4, latent_5, tile_seeds,
    anchor_parity, anchor_scale, mix_levels, mix_hidden, conv_first, conv_second,
    conv_output, context_in, context_mid, context_out,
):
    lat, lon = lax.axis_size("lat"), lax.axis_size("lon")
    lats = (latent_0, latent_1, latent_2, latent_3, latent_4, latent_5)
    fields = [pltpu.VMEM((TALL[l], WIDE[l]), F32) for l in range(LEVELS)]
    sds = jax.ShapeDtypeStruct
    packs = (sds((8, LANES), F32),) * 2
    whole = tuple(sds((TALL[l], WIDE[l]), F32) for l in range(LEVELS))
    first = ("spread", "gather", "same", "same_out", "levels", "rowof", "ctx")
    second = ("spread", "place", "tap", "tap_out")
    names = first + second[1:]
    side_near, side_far, *made = call(
        sides_kernel,
        (sds((8, 128), F32),) * 2
        + whole
        + tuple(sds((72, 3 * UPROWS[l]), BF16) for l in range(1, LEVELS))
        + tuple(sds((WIDE[l], LANES), BF16) for l in range(1, LEVELS)),
        [], [SMEM] + [HBM] * 6, 8, tile_seeds, *lats,
        forward=(
            mix_levels.T, mix_hidden, context_in.T, context_mid, context_out,
            conv_first.transpose(2, 3, 0, 1), conv_second.transpose(2, 3, 0, 1),
            conv_output.transpose(0, 2, 3, 1),
        )
        + tuple(table(n) for n in names),
    )
    quantized, scales, params = made[:6], made[6:16], made[16:24]
    held = dict(zip(names, made[24:]))
    pair = [(i, i ^ 1) for i in range(lon)]
    other = [(i, (i + 1) % lon if i & 1 else (i - 1) % lon) for i in range(lon)]
    side_far = lax.ppermute(side_far, "lon", other)
    side_near = lax.ppermute(side_near, "lon", pair)
    token, wm1, wm2, a1, a2, a3 = call(
        mix_weights_kernel,
        (
            sds((8, 128), F32), sds((BLOCK, 48), BF16), sds((BLOCK, BLOCK), BF16),
            sds((BLOCK, 240), BF16), sds((PAIR, 3 * PAIR), BF16), sds((16, 3 * BLOCK), BF16),
        ),
        [], [VMEM] * (5 + len(first)), 4, *params[:5], *[held[n] for n in first],
    )
    end_near, end_far = call(
        ends_kernel, packs, [pltpu.VMEM((8, LANES), F32)] * 2, [VMEM] * 9, 4,
        *quantized, side_near, side_far, token,
    )
    pair = [(i, i ^ 1) for i in range(lat)]
    other = [(i, i + 1 if i & 1 else i - 1) for i in range(1, lat - 1)]
    end_far = lax.ppermute(end_far, "lat", other)
    end_near = lax.ppermute(end_near, "lat", pair)
    wc1, wc2, wout = call(
        conv_weights_kernel,
        (sds((HALF, 3 * SHORT), BF16), sds((HALF, 3 * SHORT), BF16), sds((72, SLAB), F32)),
        [], [VMEM] * (3 + len(second)), 4, *params[5:], *[held[n] for n in second],
    )

    pixels = float(3 * H * W * lat * lon)
    feature = pltpu.VMEM((3, 2 * EDGE + BLOCK * BLOCKS, LANES), BF16)
    hidden = pltpu.VMEM((UNITS + 1, 2 * BLOCK, W), BF16)
    plain = pltpu.VMEM((UNITS + 1, 8, W), F32)
    fields = [pltpu.VMEM((TALL[l], WIDE[l]), F32) for l in range(LEVELS)]
    recon, bits, part = call(
        functools.partial(main_kernel, pixels=pixels, lat=lat),
        (sds((3, H, W), F32), sds((H, W), F32), sds((16, 128), F32)),
        [pltpu.VMEM((3, H, W), F32), pltpu.VMEM((H, W), F32), pltpu.SemaphoreType.DMA((2,))]
        + fields
        + [pltpu.VMEM((48 * BLOCKS, LANES), F32), feature, feature]
        + [pltpu.VMEM((UNITS + 1, 160, W), BF16), hidden, hidden, plain, plain]
        + [pltpu.VMEM((8, 80, LANES), BF16), pltpu.VMEM((8, W), F32)],
        [SCALARS] * 2 + [VMEM] * 10 + [HBM] + [VMEM] * 18,
        40,
        anchor_parity, anchor_scale, *quantized, side_near, side_far, end_near, end_far, target,
        wm1, wm2, wc1, wc2, wout, a1, a2, a3,
        *scales,
        out_specs=(HBM, HBM, VMEM),
    )
    steps = pair_steps(lat, lon)
    for step in steps[:-1]:
        part = part + lax.ppermute(part, ("lat", "lon"), step)
    other = lax.ppermute(part, ("lat", "lon"), steps[-1])
    sizes = [pixels] + [float(ROWS[l] * COLS[l] * lat * lon) for l in range(LEVELS)]
    loss, grad = call(
        functools.partial(final_kernel, sizes=sizes),
        (sds((1, 7), F32), sds((3, 3, 3, CH), F32)), [], [VMEM] * 2, 1, part, other,
    )
    return recon, bits, loss.reshape(7), grad.transpose(0, 3, 1, 2)


def solution(mesh):
    tile = P("lat", "lon")
    return jax.shard_map(
        local,
        mesh=mesh,
        in_specs=(P(None, "lat", "lon"),) + (tile,) * 7 + (P(),) * 10,
        out_specs=(P(None, "lat", "lon"), tile, P(), P()),
        check_vma=False,
    )
```

```python
import functools

import jax
import jax.numpy as jnp
import numpy as np
from jax import lax
from jax.experimental import pallas as pl
from jax.experimental.pallas import tpu as pltpu
from jax.sharding import PartitionSpec as P


F32, BF16, I32 = jnp.float32, jnp.bfloat16, jnp.int32
STEPS = (
    (-1, 0), (1, 0), (0, -1), (0, 1), (-2, -1), (-2, 1),
    (2, -1), (2, 1), (-1, -2), (-1, 2), (1, -2), (1, 2),
)
LEVELS, CH, H, W = 6, 24, 64, 512
ROWS = [H >> l for l in range(LEVELS)]
COLS = [W >> l for l in range(LEVELS)]
HALO = [3, 2, 2, 2, 2, 2]
OFFS = [0, 3, 5, 7, 9, 11]
PACK = 13
WIDE = [640, 384, 256, 128, 128, 128]
TALL = [80, 56, 40, 32, 32, 32]
TOP = 12
UPROWS = [0, 48, 32, 16, 16, 16]
LANES = 640
BLOCKS = 9
BLOCK = 8 * CH
SLAB = 256
HALF = 4 * CH
PAIR = 2 * CH
SHORT = 160
UNITS = 11
EARLY = range(1, 6)
LATE = [u for u in range(UNITS) if u not in EARLY]
LAST = [(3, 0), (4, 64), (5, 96)]
EDGE = 32
PLACE = [(0, 0), (3, 0), (3, 384), (5, 0), (5, 128), (5, 256)]
VMEM = pl.BlockSpec(memory_space=pltpu.VMEM)
SMEM = pl.BlockSpec(memory_space=pltpu.SMEM)
HBM = pl.BlockSpec(memory_space=pltpu.HBM)
SCALARS = pl.BlockSpec(memory_space=pltpu.HBM)


def dot(a, b):
    return lax.dot_general(a, b, (((1,), (0,)), ((), ())), preferred_element_type=F32)


def dot_t(a, b):
    return lax.dot_general(a, b, (((1,), (1,)), ((), ())), preferred_element_type=F32)


def wrap32(v):
    return int(np.int64(v).astype(np.int32))


def quantize(lat_ref, seed, level):
    shape = lat_ref.shape
    rows = lax.broadcasted_iota(I32, shape, 0)
    cols = lax.broadcasted_iota(I32, shape, 1)
    h = (seed + wrap32(level * 668265263)) + rows * 374761393 + cols * 1103515245
    h = h ^ lax.shift_right_logical(h, jnp.full(shape, 15, I32))
    h = h * 73244475
    h = h ^ lax.shift_right_logical(h, jnp.full(shape, 13, I32))
    h = h * 73244475
    h = h ^ lax.shift_right_logical(h, jnp.full(shape, 16, I32))
    noise = (h & 16777215).astype(F32) * (1.0 / 16777216.0) - 0.5
    return lat_ref[...] + noise


def place_own(lats, seed, fields):
    for level in range(LEVELS):
        fields[level][...] = jnp.zeros(fields[level].shape, F32)
        fields[level][TOP : TOP + ROWS[level], 0 : COLS[level]] = quantize(
            lats[level], seed, level
        )


def place_sides(left, right, fields):
    for level in range(LEVELS):
        base = (COLS[level] // 128) * 128
        for g in range(max(1, ROWS[level] // 8)):
            tile = side_tile(left, right, level, g)
            rows = pl.ds(TOP + 8 * g, 8)
            if base:
                fields[level][rows, base : base + 128] = tile
            else:
                fields[level][rows, 0:128] = fields[level][rows, 0:128] + tile


def place_ends(above, below, fields):
    for level in range(LEVELS):
        h, (r, c), w = HALO[level], PLACE[level], WIDE[level]
        fields[level][TOP - h : TOP, :] = above[r : r + h, c : c + w]
        end = TOP + ROWS[level]
        fields[level][end : end + h, :] = below[r : r + h, c : c + w]


def settle(copies):
    for copy in copies:
        copy.wait()


def side_tile(left, right, level, g):
    h, c = HALO[level], COLS[level]
    lane = lax.broadcasted_iota(I32, (8, 128), 1)
    start = c % 128
    at = PACK * g + OFFS[level]
    tile = jnp.where(
        (lane >= start) & (lane < start + h), pltpu.roll(right, (start - at) % 128, 1), 0.0
    )
    return jnp.where(lane >= 128 - h, pltpu.roll(left, (128 - h - at) % 128, 1), tile)


def hat(level, fine, coarse):
    place = (fine + 0.5) * (1.0 / (1 << level)) - 0.5
    return jnp.maximum(1.0 - jnp.abs(place - coarse), 0.0).astype(BF16)


def sides_kernel(copies, seed, *refs):
    lats, (near, far), fields, scales = refs[:6], refs[6:8], refs[8:14], refs[14:]
    row_scales, col_scales = scales[:5], scales[5:]
    for level in range(1, LEVELS):
        count = UPROWS[level]
        shape = (72, 3 * count)
        fine = lax.broadcasted_iota(I32, shape, 0) - 4
        at = lax.broadcasted_iota(I32, shape, 1)
        at = jnp.where(at >= 2 * count, at - 2 * count, jnp.where(at >= count, at - count, at))
        row_scales[level - 1][...] = hat(level, fine.astype(F32), (at + (8 - TOP)).astype(F32))
        own, wide, h = COLS[level], WIDE[level], HALO[level]
        for first in range(0, wide, 128):
            shape = (128, LANES)
            fine = lax.broadcasted_iota(I32, shape, 1)
            fine = jnp.where(fine < W + 4, fine, jnp.where(fine >= LANES - 4, fine - LANES, -99999))
            at = lax.broadcasted_iota(I32, shape, 0) + first
            at = jnp.where(at < own + h, at, jnp.where(at >= wide - h, at - wide, 99999))
            col_scales[level - 1][first : first + 128, :] = hat(
                level, fine.astype(F32), at.astype(F32)
            )
    settle(copies[:6])
    place_own(lats, seed[0, 0], fields)
    lane = lax.broadcasted_iota(I32, (8, 128), 1)
    right = jnp.zeros((8, 128), F32)
    left = jnp.zeros((8, 128), F32)
    for level in range(LEVELS):
        h, c = HALO[level], COLS[level]
        base = max(c - 128, 0)
        for g in range(max(1, ROWS[level] // 8)):
            at = PACK * g + OFFS[level]
            here = (lane >= at) & (lane < at + h)
            rows = pl.ds(TOP + 8 * g, 8)
            last = fields[level][rows, base : base + 128]
            first = fields[level][rows, 0:128]
            right = jnp.where(here, pltpu.roll(last, (at - (c - h - base)) % 128, 1), right)
            left = jnp.where(here, pltpu.roll(first, at % 128, 1), left)
    odd = (lax.axis_index("lon") & 1) == 1
    near[...] = jnp.where(odd, left, right)
    far[...] = jnp.where(odd, right, left)
    settle(copies[6:])


def ordered(axis, near, far):
    odd = (lax.axis_index(axis) & 1) == 1
    return jnp.where(odd, near[...], far[...]), jnp.where(odd, far[...], near[...])


def ends_kernel(copies, *refs):
    fields, sides, (_, near_out, far_out, up, down) = refs[:6], refs[6:8], refs[8:]
    left, right = ordered("lon", *sides)
    up[...] = jnp.zeros(up.shape, F32)
    down[...] = jnp.zeros(down.shape, F32)
    for level in range(LEVELS):
        h, (r, c), own = HALO[level], PLACE[level], COLS[level]
        count = max(1, ROWS[level] // 8)
        base = (own // 128) * 128
        for dst, g, skip in ((up, 0, 0), (down, count - 1, min(8, ROWS[level]) - h)):
            tile = side_tile(left, right, level, g)
            at = TOP + 8 * g + skip
            if base:
                dst[r : r + h, c : c + base] = fields[level][at : at + h, 0:base]
                dst[r : r + h, c + base : c + base + 128] = tile[skip : skip + h]
            else:
                dst[r : r + h, c : c + 128] = (
                    fields[level][at : at + h, :] + tile[skip : skip + h]
                )
    odd = (lax.axis_index("lat") & 1) == 1
    near_out[...] = jnp.where(odd, up[...], down[...])
    far_out[...] = jnp.where(odd, down[...], up[...])


def slab_row(d, c):
    return CH * d + EDGE + c


@functools.lru_cache(None)
def tables():
    t = {}
    spread = np.zeros((BLOCK, CH), np.float32)
    for r in range(8):
        for c in range(CH):
            spread[CH * r + c, c] = 1
    t["spread"] = spread
    t["gather"] = np.ascontiguousarray(spread.T)
    place = np.zeros((CH, SLAB), np.float32)
    tap = np.full((BLOCK, SLAB), 9, np.float32)
    for d in range(-1, 9):
        for c in range(CH):
            place[c, slab_row(d, c)] = 1
            for r in range(8):
                tap[CH * r : CH * r + CH, slab_row(d, c)] = d - r + 1
    t["place"], t["tap"] = place, tap
    t["tap_out"] = np.tile(tap[::CH], (3, 1))
    same = np.zeros((BLOCK, BLOCK), np.float32)
    for r in range(8):
        same[CH * r : CH * r + CH, CH * r : CH * r + CH] = 1
    t["same"] = same
    t["same_out"] = np.tile(same[::CH], (2, 1))
    levels = np.zeros((LEVELS, 8 * LEVELS), np.float32)
    rowof = np.zeros((BLOCK, 8 * LEVELS), np.float32)
    for l in range(LEVELS):
        for r in range(8):
            levels[l, 8 * l + r] = 1
            rowof[CH * r : CH * r + CH, 8 * l + r] = 1
    t["levels"], t["rowof"] = levels, rowof
    ctx = np.zeros((8, len(STEPS), 80), np.float32)
    for r in range(8):
        for k, (i, j) in enumerate(STEPS):
            ctx[r, k, (j + 2) * 16 + (r + i + 4)] = 1
    t["ctx"] = ctx
    return t


def table(name, dtype=BF16):
    return jnp.asarray(tables()[name], dtype)


def split2(x):
    hi = x.astype(BF16)
    return hi, (x - hi.astype(F32)).astype(BF16)


def split3(x):
    hi = x.astype(BF16)
    rest = x - hi.astype(F32)
    mid = rest.astype(BF16)
    return hi, mid, (rest - mid.astype(F32)).astype(BF16)


def laplace(x, centre, spread):
    y = 1.0 / spread
    off = x - centre
    mag = jnp.abs(off)
    inside = jnp.clip(off, -0.5, 0.5)
    e1 = jnp.exp((inside - 0.5) * y)
    e2 = jnp.exp((-0.5 - inside) * y)
    poly = y * (1 - y * (1 / 2 - y * (1 / 6 - y * (1 / 24 - y * (1 / 120)))))
    tail = jnp.where(y < 0.05, poly, 1.0 - e1 * e2)
    beyond = mag >= 0.5
    arg = jnp.where(beyond, 0.5 * tail, 1.0 - 0.5 * (e1 + e2))
    extra = jnp.where(beyond, (mag - 0.5) * y, 0.0)
    return (extra - jnp.log(arg)) * (1.0 / 0.6931471805599453)


def price(raw, own, plain):
    sigma = raw[8:16]
    soft = jnp.maximum(sigma, 0.0) + jnp.log(1.0 + jnp.exp(-jnp.abs(sigma)))
    anchor = plain > 0.0
    centre = jnp.where(anchor, 0.0, raw[0:8])
    return laplace(own, centre, jnp.where(anchor, plain, 0.1 + soft))


def early_units(field, parity, scale, a1, a2, a3, out):
    lane = lax.broadcasted_iota(I32, (8, W), 1)
    row = lax.broadcasted_iota(I32, (8, W), 0)
    plain = jnp.where(((row + lane + parity) & 1) == 0, scale, 0.0)
    rows = field[...]
    turned = [pltpu.roll(rows, (-j) % LANES, 1) if j else rows for j in range(-2, 3)]

    def both(value):
        hi, lo = split2(value)
        return hi, lo

    hidden = {}
    for stage in range(len(EARLY) + 2):
        if stage >= 2:
            u = EARLY[stage - 2]
            hi = jnp.concatenate([h for h, _ in hidden[u]], axis=0)
            lo = jnp.concatenate([l for _, l in hidden[u]], axis=0)
            raw = dot(a3[...], jnp.concatenate([hi, lo, hi], axis=0))
            out[u - EARLY[0]] = price(raw, rows[8 * u + 12 : 8 * u + 20, 0:W], plain)
        if 1 <= stage <= len(EARLY):
            u = EARLY[stage - 1]
            hi, lo = hidden[u]
            hidden[u] = []
            for k in range(4):
                part = slice(PAIR * k, PAIR * k + PAIR)
                deep = jnp.concatenate([hi[part], lo[part], hi[part]], axis=0)
                hidden[u].append(both(jnp.maximum(dot(a2[...], deep), 0.0)))
        if stage < len(EARLY):
            u = EARLY[stage]
            shifted = [t[8 * u + 8 : 8 * u + 24, 0:W] for t in turned]
            hi, lo = split2(jnp.concatenate(shifted, axis=0))
            inner = dot(a1[...], jnp.concatenate([hi, lo, hi], axis=0))
            hidden[u] = both(jnp.maximum(inner, 0.0))


def conv_weights_kernel(
    copies, parity, scale, q0, side_near, side_far, a1, a2, a3, cf, cs, co, spread, place, tap,
    tap_out, wc1, wc2, wout, early, field,
):
    field[...] = q0[...]
    left, right = ordered("lon", side_near, side_far)
    for g in range(H // 8):
        field[TOP + 8 * g : TOP + 8 * g + 8, W:] = side_tile(left, right, 0, g)
    grow = spread[0:HALF, :]
    short = place[:, 0:SHORT]
    taps = tap[0:HALF, 0:SHORT].astype(F32)
    for src, dst in ((cf, wc1), (cs, wc2)):
        for b in range(3):
            total = jnp.zeros((HALF, SHORT), F32)
            for a in range(3):
                full = dot(dot(grow, src[a, b]).astype(BF16), short)
                total = jnp.where(taps == float(a), full, total)
            dst[:, SHORT * b : SHORT * b + SHORT] = total.astype(BF16)
    taps3 = tap_out[...].astype(F32)[0:8]
    for o in range(3):
        rows = [dot(co[o, a], place[...]) for a in range(3)]
        for b in range(3):
            total = jnp.zeros((8, SLAB), F32)
            for a in range(3):
                line = jnp.broadcast_to(rows[a][b : b + 1], (8, SLAB))
                total = jnp.where(taps3 == float(a), line, total)
            at = 24 * b + 8 * o
            wout[at : at + 8, :] = total
    settle(copies)
    early_units(field, parity[0], scale[0], a1, a2, a3, early)


def mix_weights_kernel(
    copies, ml, mh, w1, w2, w3, spread, gather, same, same_out, levels, rowof, ctx,
    token, wm1, wm2, a1, a2, a3,
):
    settle(copies)
    token[...] = jnp.zeros(token.shape, F32)
    grow = spread[...]
    wide = gather[...]

    def diag(w):
        return dot(dot(grow, w).astype(BF16), wide) * same[...].astype(F32)

    wm1[...] = (
        dot(dot_t(grow, ml[...]).astype(BF16), levels[...]) * rowof[...].astype(F32)
    ).astype(BF16)
    wm2[...] = diag(mh[...]).astype(BF16)
    hi, lo = split2(w1[...])
    hi, lo = dot_t(grow, hi).astype(BF16), dot_t(grow, lo).astype(BF16)
    for r in range(8):
        rows = slice(CH * r, CH * r + CH)
        sel = ctx[r]
        h, l = dot(hi[rows], sel).astype(BF16), dot(lo[rows], sel).astype(BF16)
        a1[rows, :] = jnp.concatenate([h, h, l], axis=1)
    hi, lo = split2(w2[...])
    h, l = diag(hi).astype(BF16)[0:PAIR, 0:PAIR], diag(lo).astype(BF16)[0:PAIR, 0:PAIR]
    a2[...] = jnp.concatenate([h, h, l], axis=1)
    hi, lo = split2(w3[...])
    keep = same_out[...].astype(F32)

    def out(w):
        v = dot(w, wide)
        v = jnp.concatenate(
            [jnp.broadcast_to(v[0:1], (8, BLOCK)), jnp.broadcast_to(v[1:2], (8, BLOCK))], axis=0
        )
        return (v * keep).astype(BF16)

    h, l = out(hi), out(lo)
    a3[...] = jnp.concatenate([h, h, l], axis=1)


def main_kernel(
    copies, parity, scale, q0, q1, q2, q3, q4, q5, side_near, side_far, end_near, end_far, target,
    wm1, wm2, wc1, wc2, wout, a1, a2, a3, early, r1, r2, r3, r4, r5, u1, u2, u3, u4, u5,
    recon_out, bits_out, part,
    recon, bits, sems, f0, f1, f2, f3, f4, f5, up, second, third, taps, hidden1, hidden2, own, anchors, moved, sq,
    *, pixels, lat,
):
    fields = (f0, f1, f2, f3, f4, f5)
    for src, dst in zip((q0, q1, q2, q3, q4, q5), fields):
        dst[...] = src[...]
    place_sides(*ordered("lon", side_near, side_far), fields)
    place_ends(*ordered("lat", end_near, end_far), fields)

    for n in range(BLOCKS):
        up[48 * n : 48 * n + 8, :] = f0[8 + 8 * n : 16 + 8 * n, :]
    for level, ru, cu in ((1, r1, u1), (2, r2, u2), (3, r3, u3), (4, r4, u4), (5, r5, u5)):
        count = UPROWS[level]
        grown = dot(jnp.concatenate(split3(fields[level][8 : 8 + count, :]), axis=0), cu[...])
        grown = (grown[0:count] + grown[count : 2 * count]) + grown[2 * count :]
        full = dot(ru[...], jnp.concatenate(split3(grown), axis=0))
        for n in range(BLOCKS):
            up[48 * n + 8 * level : 48 * n + 8 * level + 8, :] = full[8 * n : 8 * n + 8]

    lane = lax.broadcasted_iota(I32, (8, 128), 1)
    row = lax.broadcasted_iota(I32, (8, 128), 0)

    turned = {}
    for level in range(3):
        for j in range(-2, 3):
            rows = fields[level][8 : 24 + ROWS[level] - 8, :]
            turned[level, j] = pltpu.roll(rows, (-j) % WIDE[level], 1) if j else rows

    def turn(level, n, j):
        return turned[level, j][8 * n : 8 * n + 16, 0 : max(COLS[level], 128)]

    def small(j):
        deep = lax.broadcasted_iota(I32, (16, 128), 1)
        out = jnp.zeros((16, 128), F32)
        for level, at in LAST:
            turned = fields[level][8:24, :]
            if (at - j) % 128:
                turned = pltpu.roll(turned, (at - j) % 128, 1)
            out = jnp.where((deep >= at) & (deep < at + COLS[level]), turned, out)
        return out

    def unit(u, shifted):
        hi, lo = split2(jnp.concatenate(shifted, axis=0))
        taps[u, 0:80, :] = hi
        taps[u, 80:160, :] = lo
        own[u] = shifted[2][4:12]

    for n in range(8):
        if n not in EARLY:
            unit(n, [turn(0, n, j) for j in range(-2, 3)])
    for n in range(2):
        unit(8 + n, [
            jnp.concatenate([turn(1, 2 * n, j), turn(1, 2 * n + 1, j)], axis=1)
            for j in range(-2, 3)
        ])
    unit(10, [
        jnp.concatenate([turn(2, 0, j), turn(2, 1, j), small(j), jnp.zeros((16, 128), F32)], axis=1)
        for j in range(-2, 3)
    ])

    settle(copies[:2])

    def cover(level):
        odd = (row + lane + parity[level]) & 1
        plain = jnp.full((8, 128), scale[level], F32)
        return jnp.where(odd == 0, plain, 0.0)

    mixed = jnp.zeros((8, 128), F32)
    for level, at in LAST:
        mixed = jnp.where((lane >= at) & (lane < at + COLS[level]), cover(level), mixed)
    for u in range(UNITS):
        tiles = [cover(0 if u < 8 else 1)] * 4
        if u == 10:
            tiles = [cover(2), cover(2), mixed, mixed]
        anchors[u] = jnp.concatenate(tiles, axis=1)

    taps[UNITS] = jnp.zeros((160, W), BF16)
    own[UNITS] = jnp.zeros((8, W), F32)
    anchors[UNITS] = jnp.ones((8, W), F32)

    end = EDGE + BLOCK * BLOCKS
    for buf in (second, third):
        buf[:, 0:EDGE, :] = jnp.zeros((3, EDGE, LANES), BF16)
        buf[:, end : end + EDGE, :] = jnp.zeros((3, EDGE, LANES), BF16)
    index = lax.axis_index("lat")

    def clear(buf):
        @pl.when(index == 0)
        def _():
            buf[:, EDGE : EDGE + 96, :] = jnp.zeros((3, 96, LANES), BF16)

        @pl.when(index == lat - 1)
        def _():
            buf[:, end - 96 : end, :] = jnp.zeros((3, 96, LANES), BF16)

    def block_rows(n):
        return pl.ds(EDGE + BLOCK * n, BLOCK)

    def mix(n):
        u = up[pl.ds(48 * n, 48), :].astype(BF16)
        first = jnp.maximum(dot(wm1[...], u), 0.0).astype(BF16)
        value = jnp.maximum(dot(wm2[...], first), 0.0).astype(BF16)
        put(second, block_rows(n), value)

    def put(buf, rows, value):
        buf[1, rows, :] = value
        buf[0, rows, :] = pltpu.roll(value, 1, 1)
        buf[2, rows, :] = pltpu.roll(value, LANES - 1, 1)

    def conv(src, w, n):
        taps_of = []
        for part in range(2):
            at = BLOCK * n + HALF * part
            taps_of.append([src[b, at : at + SHORT, :] for b in range(3)])
        main = [dot(w[...], jnp.concatenate([t[:, 0:W] for t in taps], axis=0)) for taps in taps_of]
        edge = dot(
            w[...],
            jnp.concatenate(
                [
                    jnp.concatenate([taps_of[0][b][:, W:], taps_of[1][b][:, W:]], axis=1)
                    for b in range(3)
                ],
                axis=0,
            ),
        )
        out = []
        for part in range(2):
            at = EDGE + BLOCK * n + HALF * part
            rows = pl.ds(at, HALF)
            tail = edge[:, (LANES - W) * part : (LANES - W) * (part + 1)]
            c = jnp.concatenate([main[part], tail], axis=1)
            out.append((rows, (src[1, rows, :].astype(F32) + jnp.maximum(c, 0.0)).astype(BF16)))
        return out

    def conv_one(n):
        for rows, value in conv(second, wc1, n):
            put(third, rows, value)

    def conv_two(n):
        for rows, value in conv(third, wc2, n):
            second[1, rows, :] = value

    def middle(u):
        for k in range(4):
            hi = hidden1[u, PAIR * k : PAIR * k + PAIR, :]
            lo = hidden1[u, BLOCK + PAIR * k : BLOCK + PAIR * k + PAIR, :]
            out = jnp.maximum(dot(a2[...], jnp.concatenate([hi, lo, hi], axis=0)), 0.0)
            hi, lo = split2(out)
            hidden2[u, PAIR * k : PAIR * k + PAIR, :] = hi
            hidden2[u, BLOCK + PAIR * k : BLOCK + PAIR * k + PAIR, :] = lo

    def layer(src, dst, w, u, k):
        hi, lo = src[u, 0:k, :], src[u, k : 2 * k, :]
        hi, lo = split2(jnp.maximum(dot(w[...], jnp.concatenate([hi, lo, hi], axis=0)), 0.0))
        dst[u, 0:BLOCK, :] = hi
        dst[u, BLOCK : 2 * BLOCK, :] = lo

    def cost(u):
        hi, lo = hidden2[u, 0:BLOCK, :], hidden2[u, BLOCK : 2 * BLOCK, :]
        raw = dot(a3[...], jnp.concatenate([hi, lo, hi], axis=0))
        own[u] = price(raw, own[u], anchors[u])

    def run(synth, entropy):
        done = 0
        for n in range(BLOCKS):
            synth(n)
            until = (n + 1) * len(LATE) // BLOCKS
            for u in LATE[done:until]:
                entropy(u)
            done = until

    run(mix, lambda u: layer(taps, hidden1, a1, u, 80))
    clear(second)
    run(conv_one, middle)
    clear(third)
    run(conv_two, cost)
    clear(second)

    finest = jnp.zeros((8, W), F32)
    for n in range(8):
        value = early[n - EARLY[0]] if n in EARLY else own[n]
        bits[8 * n : 8 * n + 8, :] = value
        finest = finest + value

    def output(n):
        slab = second[1, BLOCK * n + 96 : BLOCK * n + 96 + SLAB, :]
        y = dot(wout[...].astype(BF16), slab)
        c = y[24:48] + pltpu.roll(y[0:24], 1, 1) + pltpu.roll(y[48:72], LANES - 1, 1)
        rows = slice(8 * n, 8 * n + 8)
        slopes = []
        total = jnp.zeros((8, W), F32)
        for o in range(3):
            value = c[8 * o : 8 * o + 8, 0:W]
            recon[o, rows, :] = value
            error = value - target[o, rows, :]
            total = total + error * error
            slopes.append((2.0 * error / pixels).astype(BF16).astype(F32))
        slope = jnp.concatenate(slopes, axis=0)
        slope = jnp.concatenate([slope, jnp.zeros((24, LANES - W), F32)], axis=1)
        moved[n, 0:72, :] = jnp.concatenate(
            [pltpu.roll(slope, LANES - 1, 1), slope, pltpu.roll(slope, 1, 1)], axis=0
        ).astype(BF16)
        return total

    settle(copies[2:3])
    send_bits = pltpu.make_async_copy(bits, bits_out, sems.at[0])
    send_bits.start()
    total = jnp.zeros((8, W), F32)
    g = jnp.zeros((72, SLAB), F32)
    for n in range(8):
        total = total + output(n)
    for n in range(8):
        g = g + dot_t(moved[n, 0:72, :], second[1, BLOCK * n + 96 : BLOCK * n + 96 + SLAB, :])
    sq[...] = total
    send_recon = pltpu.make_async_copy(recon, recon_out, sems.at[1])
    send_recon.start()
    sums = [jnp.zeros((8, W), F32)] * 2
    sums[0] = finest
    sums[1] = own[8] + own[9]
    sums.append(own[10, :, 0:128] + own[10, :, 128:256])
    for level, at in LAST:
        keep = (lane >= at) & (lane < at + COLS[level]) & (row < ROWS[level])
        sums.append(jnp.where(keep, own[10, :, 256:384], 0.0))
    row = lax.broadcasted_iota(I32, (72, SLAB), 0) & 7
    total = jnp.zeros((72, SLAB), F32)
    for r in range(8):
        total = total + jnp.where(row == r, pltpu.roll(g, (-CH * r) % SLAB, 1), 0.0)
    lane = lax.broadcasted_iota(I32, (1, 128), 1)
    rows = [
        jnp.where(
            (lane >= 8) & (lane < 8 + 3 * CH),
            jnp.sum(total[8 * k : 8 * k + 8, 0:128], axis=0, keepdims=True),
            0.0,
        )
        for k in range(9)
    ]
    lane = lax.broadcasted_iota(I32, (1, 128), 1)
    line = jnp.where(lane == 0, jnp.sum(sq[...]), 0.0)
    for level in range(LEVELS):
        line = jnp.where(lane == 1 + level, jnp.sum(sums[level]), line)
    rows[0] = rows[0] + jnp.where(lane >= 80, pltpu.roll(rows[8], 72, 1), 0.0)
    rows[1] = rows[1] + jnp.where((lane >= 80) & (lane < 104), pltpu.roll(rows[8], 24, 1), 0.0)
    rows[2] = rows[2] + jnp.where(lane >= 80, pltpu.roll(line, 80, 1), 0.0)
    for k in range(8):
        part[k : k + 1, :] = rows[k]
    send_bits.wait()
    send_recon.wait()


def final_kernel(copies, mine, other, loss, grad, *, sizes):
    total = mine[...] + other[...]
    lane = lax.broadcasted_iota(I32, (1, 7), 1)
    size = jnp.full((1, 7), sizes[0], F32)
    for k in range(1, 7):
        size = jnp.where(lane == k, sizes[k], size)
    loss[...] = pltpu.roll(total, 128 - 80, 1)[2:3, 0:7] / size
    wide = lax.broadcasted_iota(I32, (1, 128), 1)
    ninth = jnp.where(
        wide < 56, pltpu.roll(total, 128 - 72, 1)[0:1], pltpu.roll(total, 128 - 24, 1)[1:2]
    )
    total = jnp.concatenate([total, jnp.broadcast_to(ninth, (8, 128))], axis=0)
    for a in range(3):
        turned = pltpu.roll(total, 128 - 8 - CH * a, 1)
        for b in range(3):
            for o in range(3):
                k = 3 * b + o
                grad[o, a, b : b + 1, :] = turned[k : k + 1, 0:CH]


def pair_steps(lat, lon):
    def flat(f):
        return [(a * lon + b, f(a, b)[0] * lon + f(a, b)[1]) for a in range(lat) for b in range(lon)]

    steps = []
    if (lat, lon) == (8, 32):
        def ring4(v, odd):
            return v ^ 1 if not odd else ((v + 1) % 4 if v & 1 else (v - 1) % 4)

        def far8(z):
            return {1: 6, 6: 1, 2: 5, 5: 2, 3: 0, 0: 3, 4: 7, 7: 4}[z]

        def y_move(a, b, odd):
            y = ring4((a // 4) * 2 + ((b // 2) & 1), odd)
            return (y // 2) * 4 + a % 4, (b & ~2) | ((y & 1) << 1)

        def z_move(a, b, f):
            return a, f(b // 4) * 4 + b % 4

        steps.append(flat(lambda a, b: (a, b ^ 1)))
        for odd in (False, True):
            steps.append(flat(lambda a, b, odd=odd: ((a & ~3) | ring4(a & 3, odd), b)))
        for odd in (False, True):
            steps.append(flat(lambda a, b, odd=odd: y_move(a, b, odd)))
        steps.append(flat(lambda a, b: z_move(a, b, lambda z: z ^ 1)))
        steps.append(flat(lambda a, b: z_move(a, b, lambda z: (z + 1) % 8 if z & 1 else (z - 1) % 8)))
        steps.append(flat(lambda a, b: z_move(a, b, far8)))
        return steps
    k = 1
    while k < lon:
        steps.append(flat(lambda a, b, k=k: (a, b ^ k)))
        k *= 2
    k = 1
    while k < lat:
        steps.append(flat(lambda a, b, k=k: (a ^ k, b)))
        k *= 2
    return steps


def call(kernel, outs, scratch, specs, mib, *args, out_specs=None, forward=()):
    own = len(args)
    args = args + tuple(forward)
    specs = specs + [HBM] * len(forward)
    outs = outs + tuple(jax.ShapeDtypeStruct(a.shape, a.dtype) for a in forward)
    held = [i for i, spec in enumerate(specs) if spec is HBM or spec is SCALARS]
    many = len(jax.tree.leaves(outs))

    def body(*refs):
        args_in, rest = list(refs[: len(specs)]), refs[len(specs) :]
        outs_in, work = rest[:many], rest[many:]
        bufs, sems, work = work[: inner], work[inner], work[inner + 1 :]
        bufs = list(bufs) + list(outs_in[many - len(forward) :])
        copies = []
        for k, i in enumerate(held):
            copy = pltpu.make_async_copy(args_in[i], bufs[k], sems.at[k])
            copy.start()
            copies.append(copy)
            args_in[i] = bufs[k]
        kernel(copies, *args_in[:own], *outs_in[: many - len(forward)], *work)

    args = [
        pltpu.with_memory_space_constraint(a, pltpu.HBM) if spec is HBM or spec is SCALARS else a
        for a, spec in zip(args, specs)
    ]
    space = {i: pltpu.SMEM if specs[i] is SCALARS else pltpu.VMEM for i in held}
    buffers = [space[i](args[i].shape, args[i].dtype) for i in held if i < own]
    inner = len(buffers)
    return pl.pallas_call(
        body,
        out_shape=outs,
        in_specs=specs,
        out_specs=out_specs or jax.tree.map(lambda _: VMEM, outs),
        scratch_shapes=buffers + [pltpu.SemaphoreType.DMA((max(1, len(held)),))] + list(scratch),
        compiler_params=pltpu.CompilerParams(vmem_limit_bytes=mib * 1024 * 1024),
    )(*args)


def local(
    target, latent_0, latent_1, latent_2, latent_3, latent_4, latent_5, tile_seeds,
    anchor_parity, anchor_scale, mix_levels, mix_hidden, conv_first, conv_second,
    conv_output, context_in, context_mid, context_out,
):
    lat, lon = lax.axis_size("lat"), lax.axis_size("lon")
    lats = (latent_0, latent_1, latent_2, latent_3, latent_4, latent_5)
    fields = [pltpu.VMEM((TALL[l], WIDE[l]), F32) for l in range(LEVELS)]
    sds = jax.ShapeDtypeStruct
    packs = (sds((8, LANES), F32),) * 2
    whole = tuple(sds((TALL[l], WIDE[l]), F32) for l in range(LEVELS))
    first = ("spread", "gather", "same", "same_out", "levels", "rowof", "ctx")
    second = ("spread", "place", "tap", "tap_out")
    names = first + second[1:]
    side_near, side_far, *made = call(
        sides_kernel,
        (sds((8, 128), F32),) * 2
        + whole
        + tuple(sds((72, 3 * UPROWS[l]), BF16) for l in range(1, LEVELS))
        + tuple(sds((WIDE[l], LANES), BF16) for l in range(1, LEVELS)),
        [], [SMEM] + [HBM] * 6, 8, tile_seeds, *lats,
        forward=(
            mix_levels.T, mix_hidden, context_in.T, context_mid, context_out,
            conv_first.transpose(2, 3, 0, 1), conv_second.transpose(2, 3, 0, 1),
            conv_output.transpose(0, 2, 3, 1),
        )
        + tuple(table(n) for n in names),
    )
    quantized, scales, params = made[:6], made[6:16], made[16:24]
    held = dict(zip(names, made[24:]))
    pair = [(i, i ^ 1) for i in range(lon)]
    other = [(i, (i + 1) % lon if i & 1 else (i - 1) % lon) for i in range(lon)]
    side_far = lax.ppermute(side_far, "lon", other)
    side_near = lax.ppermute(side_near, "lon", pair)
    token, wm1, wm2, a1, a2, a3 = call(
        mix_weights_kernel,
        (
            sds((8, 128), F32), sds((BLOCK, 48), BF16), sds((BLOCK, BLOCK), BF16),
            sds((BLOCK, 240), BF16), sds((PAIR, 3 * PAIR), BF16), sds((16, 3 * BLOCK), BF16),
        ),
        [], [VMEM] * (5 + len(first)), 4, *params[:5], *[held[n] for n in first],
    )
    end_near, end_far = call(
        ends_kernel, packs, [pltpu.VMEM((8, LANES), F32)] * 2, [VMEM] * 9, 4,
        *quantized, side_near, side_far, token,
    )
    pair = [(i, i ^ 1) for i in range(lat)]
    other = [(i, i + 1 if i & 1 else i - 1) for i in range(1, lat - 1)]
    end_far = lax.ppermute(end_far, "lat", other)
    end_near = lax.ppermute(end_near, "lat", pair)
    wc1, wc2, wout, early = call(
        conv_weights_kernel,
        (
            sds((HALF, 3 * SHORT), BF16), sds((HALF, 3 * SHORT), BF16), sds((72, SLAB), F32),
            sds((len(EARLY), 8, W), F32),
        ),
        [pltpu.VMEM((TALL[0], LANES), F32)],
        [SCALARS] * 2 + [VMEM] * (9 + len(second)), 16, anchor_parity, anchor_scale, quantized[0],
        side_near, side_far, a1, a2, a3, *params[5:], *[held[n] for n in second],
    )

    pixels = float(3 * H * W * lat * lon)
    feature = pltpu.VMEM((3, 2 * EDGE + BLOCK * BLOCKS, LANES), BF16)
    hidden = pltpu.VMEM((UNITS + 1, 2 * BLOCK, W), BF16)
    plain = pltpu.VMEM((UNITS + 1, 8, W), F32)
    fields = [pltpu.VMEM((TALL[l], WIDE[l]), F32) for l in range(LEVELS)]
    recon, bits, part = call(
        functools.partial(main_kernel, pixels=pixels, lat=lat),
        (sds((3, H, W), F32), sds((H, W), F32), sds((8, 128), F32)),
        [pltpu.VMEM((3, H, W), F32), pltpu.VMEM((H, W), F32), pltpu.SemaphoreType.DMA((2,))]
        + fields
        + [pltpu.VMEM((48 * BLOCKS, LANES), F32), feature, feature]
        + [pltpu.VMEM((UNITS + 1, 160, W), BF16), hidden, hidden, plain, plain]
        + [pltpu.VMEM((8, 80, LANES), BF16), pltpu.VMEM((8, W), F32)],
        [SCALARS] * 2 + [VMEM] * 10 + [HBM] + [VMEM] * 19,
        40,
        anchor_parity, anchor_scale, *quantized, side_near, side_far, end_near, end_far, target,
        wm1, wm2, wc1, wc2, wout, a1, a2, a3, early,
        *scales,
        out_specs=(HBM, HBM, VMEM),
    )
    steps = pair_steps(lat, lon)
    for step in steps[:-1]:
        part = part + lax.ppermute(part, ("lat", "lon"), step)
    other = lax.ppermute(part, ("lat", "lon"), steps[-1])
    sizes = [pixels] + [float(ROWS[l] * COLS[l] * lat * lon) for l in range(LEVELS)]
    loss, grad = call(
        functools.partial(final_kernel, sizes=sizes),
        (sds((1, 7), F32), sds((3, 3, 3, CH), F32)), [], [VMEM] * 2, 1, part, other,
    )
    return recon, bits, loss.reshape(7), grad.transpose(0, 3, 1, 2)


def solution(mesh):
    tile = P("lat", "lon")
    return jax.shard_map(
        local,
        mesh=mesh,
        in_specs=(P(None, "lat", "lon"),) + (tile,) * 7 + (P(),) * 10,
        out_specs=(P(None, "lat", "lon"), tile, P(), P()),
        check_vma=False,
    )
```
